32 devices in a mesh: rows: 8 (over y, x, core), rhs: 4 (over z).
Axes of the slice: x: 2, y: 2, z: 4, core: 2. Of those that a mesh axis runs over, the one named last changes fastest.
Arguments:
- samples: float32 [65536, 16], P(('rows', 'rhs')), may hold values from -5 to 5
- freq_table: float32 [4096, 16], replicated, may hold values from -3 to 3
- feature_seeds: int32 [512], replicated, may hold values from 0 to 4095
- phases: float32 [512], replicated, may hold values from -3.140625 to 3.140625
- treatment_features: bfloat16 [65536, 512], P('rows', 'rhs'), may hold values from -2.5 to 2.5, as said below
Outputs:
- coefficients: float32 [512, 512], replicated
- fitted: float32 [65536, 512], P(('rows', 'rhs'))
The draws below stay inside these ranges and needn't reach their ends.
Inputs may be any that keep to these rules, and one draw needn't show every extreme that they name: `treatment_features`: treatment features depend on the instrument values.
All inputs are finite; a program needn't handle non-finite values.
Results may differ from the reference program's by a relative error of at most 0.0008.
The reference program's roundings to bfloat16 on the way count: a program that leaves them out, or rounds other values in their place, can miss the bound.
Values may be sent and summed in bfloat16 or wider, within the bound.
A program may use at most 64 MiB of HBM per device.

```python
import jax
import jax.numpy as jnp
from jax import lax

M = 512
P_SIZE = 512
DX = 16
NFREQ = 4096
TOTAL = 65536


def joint_values(key):
    base = jax.random.fold_in(key, 7)
    values = jnp.clip(jax.random.normal(jax.random.fold_in(base, 1), (TOTAL, DX), jnp.float32), -5.0, 5.0)
    mixing = jax.random.normal(jax.random.fold_in(base, 2), (DX, P_SIZE), jnp.float32) * 0.4
    noise = jax.random.normal(jax.random.fold_in(base, 3), (TOTAL, P_SIZE), jnp.float32)
    targets = jnp.clip(jnp.tanh(jnp.dot(values, mixing)) + 0.3 * noise, -2.5, 2.5)
    return (values, targets)


def draw_samples(key, part):
    return joint_values(key)[0]


def draw_treatment_features(key, part):
    return joint_values(key)[1].astype(jnp.bfloat16)


def plant(array, stream_key, least, top_value):
    longest = array.shape.index(max(array.shape))
    spots = []
    for shift in (0, 1):
        where = [jax.random.randint(jax.random.fold_in(stream_key, axis), (), 0, length) for axis, length in enumerate(array.shape)]
        where[longest] = (where[longest] + shift) % array.shape[longest]
        spots.append(tuple(where))
    return array.at[spots[0]].set(least).at[spots[1]].set(top_value)


def gaussian(rng, extent, deviation, reach, kind=jnp.bfloat16):
    entries = deviation * jax.random.normal(rng, extent, jnp.float32)
    return jnp.clip(entries, min=-reach, max=reach).astype(kind)


def setup_inputs(seed: int = 0) -> dict:
    streams_of = jax.random.split(jax.random.key(seed), 6)
    return {
        "samples": draw_samples(jax.random.fold_in(streams_of[5], 71), 0),
        "freq_table": gaussian(streams_of[1], (NFREQ, DX), 0.5, 3.0, jnp.float32),
        "feature_seeds": plant(jax.random.randint(streams_of[2], (M,), 0, NFREQ), jax.random.fold_in(streams_of[2], 1), 0, NFREQ - 1).astype(jnp.int32),
        "phases": jnp.clip(jax.random.uniform(streams_of[3], (M,), jnp.float32, -3.140625, 3.140625), -3.140625, 3.140625),
        "treatment_features": draw_treatment_features(jax.random.fold_in(streams_of[5], 71), 0),
    }


ridge = 0.05

def solve_with(factor, right):
    lower = lax.linalg.triangular_solve(factor, right, left_side=True, lower=True)
    return lax.linalg.triangular_solve(factor, lower, left_side=True, lower=True, transpose_a=True)

def reference(samples, freq_table, feature_seeds, phases, treatment_features):
    count = samples.shape[0]
    freqs = freq_table[feature_seeds.astype(jnp.int32)]
    angles = jnp.dot(samples.astype(jnp.float32), freqs.T.astype(jnp.float32), precision=lax.Precision.HIGHEST, preferred_element_type=jnp.float32) + phases
    instruments = (jnp.sqrt(jnp.float32(2.0)) * jnp.cos(angles)).astype(jnp.bfloat16)
    gram = jnp.dot(instruments.T.astype(jnp.float32), instruments.astype(jnp.float32), preferred_element_type=jnp.float32) / count
    gram = gram + ridge * jnp.eye(gram.shape[0], dtype=jnp.float32)
    cross = jnp.dot(instruments.T.astype(jnp.float32), treatment_features.astype(jnp.float32), preferred_element_type=jnp.float32) / count
    factor = jnp.linalg.cholesky(gram)
    coefficients = solve_with(factor, cross)
    fitted = jnp.dot(instruments.astype(jnp.float32), coefficients.astype(jnp.bfloat16).astype(jnp.float32), preferred_element_type=jnp.float32)
    return (coefficients, fitted)
```

```python
import functools
import math

import jax
import jax.numpy as jnp
from jax import lax
from jax.experimental import pallas as pl
from jax.experimental.pallas import tpu as pltpu
from jax.sharding import PartitionSpec as P

ridge = 0.05
MESH = pl.DeviceIdType.MESH
HIGHEST = lax.Precision.HIGHEST
VMEM = pl.BlockSpec(memory_space=pltpu.VMEM)
ANY = pl.BlockSpec(memory_space=pl.ANY)
TILE = 128
SIN_TERMS = [3.141592580044735, -5.1677068789267455, 2.550031377285281, -0.598045174146624, 0.07722012899537994]


def split_low(x):
    high = lax.reduce_precision(x, 8, 7)
    rest = x - high
    middle = lax.reduce_precision(rest, 8, 7)
    low = rest - middle
    return tuple(t.astype(jnp.bfloat16) for t in (high, middle, low))


def features(x, f):
    high = x.astype(jnp.bfloat16)
    left = x - high.astype(jnp.float32)
    middle = left.astype(jnp.bfloat16)
    low = (left - middle.astype(jnp.float32)).astype(jnp.bfloat16)
    ones = jnp.ones(x.shape, jnp.bfloat16)
    rows = jnp.concatenate([high, high, middle, middle, high, low, ones], axis=0)
    turns = jnp.dot(f, rows, preferred_element_type=jnp.float32)
    r = turns - jnp.round(turns)
    u = r * r
    scale = math.sqrt(2.0 * math.sqrt(2.0))
    s = u * (SIN_TERMS[-1] * scale) + SIN_TERMS[-2] * scale
    for term in reversed(SIN_TERMS[:-2]):
        s = s * u + term * scale
    s = s * r
    return (math.sqrt(2.0) - s * s).astype(jnp.bfloat16)


def exchange(R, Z, count, w_ref, got, out, sems):
    send, recv, zsend, zrecv, psend, precv, csend, crecv = sems
    r, z = lax.axis_index("rows"), lax.axis_index("rhs")
    core, spot, half = lax.rem(r, 2), r // 2, R // 2

    def copy(src, dst, out_sem, in_sem, d, peer):
        return pltpu.make_async_remote_copy(
            src_ref=src,
            dst_ref=dst,
            send_sem=out_sem.at[d],
            recv_sem=in_sem.at[d],
            device_id=peer,
            device_id_type=MESH,
        )

    def scatter(d):
        peer = lax.rem(r + d, R)
        return copy(w_ref.at[peer], got.at[d], send, recv, d, {"rows": peer})

    def along(d):
        mine = out.at[r, z]
        return copy(mine, mine, zsend, zrecv, d, {"rhs": lax.rem(z + d, Z)})

    def across(d):
        peer = lax.rem(spot + d, half) * 2 + core
        return copy(out.at[r], out.at[r], psend, precv, d, {"rows": peer})

    def aside(d):
        where = out.at[lax.rem(spot - d + half, half) * 2 + core]
        return copy(where, where, csend, crecv, d, {"rows": r + 1 - 2 * core})

    def first():
        for d in range(1, R):
            scatter(d).start()

    def second():
        total = w_ref[r]
        for d in range(1, R):
            scatter(d).wait()
            total = total + got[d]
        out[r, z] = total * (1.0 / count)
        for d in range(1, Z):
            along(d).start()

    def third():
        for d in range(1, Z):
            along(d).wait()
        for d in range(1, half):
            across(d).start()
        aside(0).start()

    def fourth():
        for d in range(1, half):
            across(d).wait()
            aside(d).start()

    def last():
        for d in range(half):
            aside(d).wait()

    return first, second, third, fourth, last


def invert_block(ref, dst):
    groups = TILE // 8
    a = [ref[8 * i : 8 * i + 8, :] for i in range(groups)]
    lane = lax.broadcasted_iota(jnp.int32, (8, TILE), 1)
    sub = lax.broadcasted_iota(jnp.int32, (8, TILE), 0)

    def across(v, j):
        return jnp.broadcast_to(v[:, j : j + 1], (8, TILE))

    def down(v, i):
        return jnp.broadcast_to(v[i : i + 1, :], (8, TILE))

    for g in range(groups):
        k = 8 * g
        c = [0.0 - across(a[g], k + j) for j in range(8)]
        far = [[across(a[i], k + j) if i != g else None for i in range(groups)] for j in range(8)]
        inside = jnp.logical_and(lane >= k, lane < k + 8)
        rows = jnp.where(inside, jnp.where(lane == sub + k, 1.0, 0.0), a[g])
        for s in range(0, 8, 2):
            p, q, r = down(c[s], s), down(c[s + 1], s), down(c[s + 1], s + 1)
            scale = 1.0 / (p * r - q * q)
            e0, e1, e2 = r * scale, -q * scale, p * scale
            pair = jnp.logical_and(sub >= s, sub < s + 2)
            l0 = jnp.where(pair, jnp.where(sub == s, 1.0, 0.0), c[s])
            l1 = jnp.where(pair, jnp.where(sub == s, 0.0, 1.0), c[s + 1])

            def step(v):
                v0, v1 = down(v, s), down(v, s + 1)
                w0, w1 = e0 * v0 + e1 * v1, e1 * v0 + e2 * v1
                return jnp.where(pair, 0.0, v) - (l0 * w0 + l1 * w1)

            rows = step(rows)
            for j in range(s + 2, 8):
                c[j] = step(c[j])
        w = [down(rows, i) for i in range(8)]
        for i in range(groups):
            if i == g:
                continue
            f = [far[j][i] * w[j] for j in range(8)]
            total = ((f[0] + f[1]) + (f[2] + f[3])) + ((f[4] + f[5]) + (f[6] + f[7]))
            a[i] = jnp.where(inside, 0.0, a[i]) - total
        a[g] = rows
    for i in range(groups):
        dst[8 * i : 8 * i + 8, :] = a[i]


def fused_kernel(
    R, Z, parts, count, x_ref, f_ref, t_hbm, coef_ref, low_ref, own_hbm,
    xs, t_ref, own, turned, acc, w, got, out, v, vgot, vout,
    gram, upper, lower, right, inverse, inner, send, recv, local, *rest
):
    phis, sems = rest[:parts], rest[parts:]
    r, z = lax.axis_index("rows"), lax.axis_index("rhs")
    size, panel = acc.shape
    chunk = x_ref.shape[1] // parts
    blocks = size // TILE
    load = pltpu.make_async_copy(t_hbm, t_ref, local.at[0])
    load.start()
    barrier = pltpu.get_barrier_semaphore()
    for d in range(1, R):
        pl.semaphore_signal(
            barrier, inc=1, device_id={"rows": lax.rem(r + d, R)}, device_id_type=MESH
        )
    for d in range(1, Z):
        pl.semaphore_signal(
            barrier, inc=1, device_id={"rhs": lax.rem(z + d, Z)}, device_id_type=MESH
        )
    pl.semaphore_wait(barrier, R + Z - 2)

    def moving(q, way):
        block, part = z - way * (q // parts), lax.rem(q, parts)
        if isinstance(q, int):
            source = x_ref.at[:, q * chunk : (q + 1) * chunk]
        else:
            source = xs.at[block, part]
        return pltpu.make_async_remote_copy(
            src_ref=source,
            dst_ref=xs.at[block, part],
            send_sem=send.at[(way + 1) // 2, q],
            recv_sem=recv.at[(way + 1) // 2, q],
            device_id={"rhs": z + way},
            device_id_type=MESH,
        )

    def arriving(q, way):
        block, part = z - way * (q // parts + 1), lax.rem(q, parts)
        return pltpu.make_async_remote_copy(
            src_ref=xs.at[block, part],
            dst_ref=xs.at[block, part],
            send_sem=send.at[(way + 1) // 2, q],
            recv_sem=recv.at[(way + 1) // 2, q],
            device_id={"rhs": z - way},
            device_id_type=MESH,
        )

    def inside(p):
        return jnp.logical_and(p >= 0, p < Z)

    for q in range(parts):
        for way in (1, -1):
            pl.when(inside(z + way))(lambda: moving(q, way).start())
    for part in range(parts):
        xs[z, part] = x_ref[:, part * chunk : (part + 1) * chunk]
    acc[...] = jnp.zeros_like(acc)
    near = jnp.minimum(z, Z - 1 - z)

    @pl.loop(0, Z)
    def _(d):
        for part in range(parts):
            q = (d - 1) * parts + part
            for way in (1, -1):

                @pl.when(jnp.logical_and(d > 0, inside(z - way * d)))
                def _():
                    arriving(q, way).wait_recv()
                    pl.when(inside(z + way))(lambda: moving(q + parts, way).start())

        step = (d + 1) // 2
        both = jnp.where(d % 2 == 1, z - step, z + step)
        single = jnp.where(z < Z - 1 - z, z + d - near, z - d + near)
        block = jnp.where(d <= 2 * near, both, single)
        for part, phi in enumerate(phis):
            phi[block] = features(xs[block, part], f_ref[...])
            mine = phi[block, pl.ds(pl.multiple_of(z * panel, panel), panel), :]
            turned[part] = mine.T
            acc[...] += jnp.dot(phi[block], turned[part], preferred_element_type=jnp.float32)

    @pl.loop(0, Z * parts)
    def _(q):
        for way in (1, -1):
            sent = jnp.logical_and(inside(z + way), inside(z - way * (q // parts)))
            pl.when(sent)(lambda: moving(q, way).wait_send())

    stages = [
        exchange(R, Z, count, w.at[c], got.at[c], out.at[c], [s.at[c] for s in sems[:8]])
        for c in range(blocks)
    ]
    rows = TILE // R
    for c in range(blocks):
        for i in range(R):
            at = c * TILE + i * rows
            w[c, i] = acc[at : at + rows, :]
        stages[c][0]()
    load.wait()
    acc[...] = jnp.zeros_like(acc)

    def cross(low, high):
        @pl.loop(low, high)
        def _(block):
            for part, phi in enumerate(phis):
                here = pl.multiple_of((block * parts + part) * chunk, chunk)
                acc[...] += jnp.dot(
                    phi[block], t_ref[pl.ds(here, chunk), :], preferred_element_type=jnp.float32
                )

    def keep(part):
        own[part] = phis[part][z].T
        pltpu.make_async_copy(own.at[part], own_hbm.at[part], local.at[1 + part]).start()

    def spread(source, dest, base, height):
        for i in range(R):
            for j in range(Z):
                top = base + i * height
                dest[top : top + height, j * panel : (j + 1) * panel] = source[i, j]

    cross(0, Z // 2)
    stages[0][1]()
    cross(Z // 2, Z)
    for c in range(1, blocks):
        stages[c][1]()
    stages[0][2]()
    high = size // R
    for i in range(R):
        v[i] = acc[i * high : (i + 1) * high, :]
    last = exchange(R, Z, count, v, vgot, vout, sems[8:])
    last[0]()
    for c in range(1, blocks):
        stages[c][2]()
    for part in range(parts):
        keep(part)
    stages[0][3]()
    for c in range(1, blocks):
        stages[c][3]()
    stages[0][4]()
    spread(out.at[0], gram, 0, rows)
    row = lax.broadcasted_iota(jnp.int32, (TILE, TILE), 0)
    col = lax.broadcasted_iota(jnp.int32, (TILE, TILE), 1)
    eye = jnp.where(row == col, jnp.float32(ridge), 0.0)
    dot = functools.partial(jnp.dot, precision=HIGHEST, preferred_element_type=jnp.float32)

    def at(i):
        return slice(i * TILE, (i + 1) * TILE)

    @pl.loop(0, blocks)
    def _(k):
        mine = pl.ds(pl.multiple_of(k * TILE, TILE), TILE)

        @pl.loop(0, k)
        def _(i):
            above = pl.ds(pl.multiple_of(i * TILE, TILE), TILE)
            left = upper[above, mine].T
            lower[mine, above] = left
            gram[mine, :] -= dot(left, gram[above, :])

        upper[mine, :] = gram[mine, :]
        inner[...] = gram[mine, mine] + eye
        invert_block(inner, inverse.at[k])
        gram[mine, :] = dot(inverse[k], upper[mine, :])
        for c in range(1, blocks):

            @pl.when(k == c - 1)
            def _():
                stages[c][4]()
                spread(out.at[c], gram, c * TILE, rows)

        for i, stage in enumerate(last[1:]):
            pl.when(k == min(i, blocks - 1))(stage)

    spread(vout, right, 0, high)
    for k in range(blocks):
        value = right[at(k), :]
        if k:
            value -= dot(lower[at(k), : k * TILE], right[: k * TILE, :])
        right[at(k), :] = dot(inverse[k], value)
    for k in reversed(range(blocks)):
        value = right[at(k), :]
        if k + 1 < blocks:
            value -= dot(gram[at(k), (k + 1) * TILE :], coef_ref[(k + 1) * TILE :, :])
        coef_ref[at(k), :] = value
        low_ref[at(k), :] = value.astype(jnp.bfloat16)
    for part in range(parts):
        pltpu.make_async_copy(own.at[part], own_hbm.at[part], local.at[1 + part]).wait()


def fused(x, freqs, targets):
    R, Z = lax.axis_size("rows"), lax.axis_size("rhs")
    depth, length = x.shape
    size = freqs.shape[0]
    panel = targets.shape[1]
    columns = Z * panel
    chunk = min(length, 512)
    parts = length // chunk
    blocks = size // TILE
    rows, high = TILE // R, size // R
    sems = pltpu.SemaphoreType.DMA
    f32, bf16 = jnp.float32, jnp.bfloat16
    return pl.pallas_call(
        functools.partial(fused_kernel, R, Z, parts, length * R * Z),
        out_shape=[
            jax.ShapeDtypeStruct((size, columns), f32),
            jax.ShapeDtypeStruct((size, columns), bf16),
            jax.ShapeDtypeStruct((parts, chunk, size), bf16),
        ],
        in_specs=[VMEM, VMEM, ANY],
        out_specs=[VMEM, VMEM, ANY],
        scratch_shapes=[
            pltpu.VMEM((Z, parts, depth, chunk), f32),
            pltpu.VMEM(targets.shape, targets.dtype),
            pltpu.VMEM((parts, chunk, size), bf16),
            pltpu.VMEM((parts, chunk, panel), bf16),
            pltpu.VMEM((size, panel), f32),
            pltpu.VMEM((blocks, R, rows, panel), f32),
            pltpu.VMEM((blocks, R, rows, panel), f32),
            pltpu.VMEM((blocks, R, Z, rows, panel), f32),
            pltpu.VMEM((R, high, panel), f32),
            pltpu.VMEM((R, high, panel), f32),
            pltpu.VMEM((R, Z, high, panel), f32),
            pltpu.VMEM((size, size), f32),
            pltpu.VMEM((size, size), f32),
            pltpu.VMEM((size, size), f32),
            pltpu.VMEM((size, columns), f32),
            pltpu.VMEM((blocks, TILE, TILE), f32),
            pltpu.VMEM((TILE, TILE), f32),
            sems((2, Z * parts)),
            sems((2, Z * parts)),
            sems((1 + parts,)),
        ]
        + [pltpu.VMEM((Z, size, chunk), bf16)] * parts
        + [sems((blocks, R))] * 2 + [sems((blocks, Z))] * 2 + [sems((blocks, R))] * 4
        + [sems((R,))] * 2 + [sems((Z,))] * 2 + [sems((R,))] * 4,
        compiler_params=pltpu.CompilerParams(collective_id=0, has_side_effects=True),
    )(x, freqs, targets)


def fit_kernel(own_ref, low_ref, coef_ref, coef_out, fitted_ref):
    coef_out[...] = coef_ref[...]
    fitted_ref[0] = jnp.dot(own_ref[0], low_ref[...], preferred_element_type=jnp.float32)


def fit(own, low, coef):
    parts, chunk, size = own.shape
    columns = low.shape[1]
    strip = size // parts
    return pl.pallas_call(
        fit_kernel,
        grid=(parts,),
        in_specs=[
            pl.BlockSpec((1, chunk, size), lambda i: (i, 0, 0)),
            pl.BlockSpec((size, columns), lambda i: (0, 0)),
            pl.BlockSpec((strip, columns), lambda i: (i, 0)),
        ],
        out_specs=[
            pl.BlockSpec((strip, columns), lambda i: (i, 0)),
            pl.BlockSpec((1, chunk, columns), lambda i: (i, 0, 0)),
        ],
        out_shape=[
            jax.ShapeDtypeStruct((size, columns), jnp.float32),
            jax.ShapeDtypeStruct((parts, chunk, columns), jnp.float32),
        ],
    )(own, low, coef)


def body(samples, freq_table, feature_seeds, phases, treatment_features):
    turn = jnp.float32(1.0 / (2.0 * math.pi))
    high, middle, low = split_low(freq_table[feature_seeds] * turn)
    shift = jnp.stack(split_low(phases * turn), axis=1)
    shift = jnp.pad(shift, ((0, 0), (0, high.shape[1] - shift.shape[1])))
    freqs = jnp.concatenate([high, middle, high, middle, low, high, shift], axis=1)
    coef, low_coef, own = fused(samples.T, freqs, treatment_features)
    coefficients, fitted = fit(own, low_coef, coef)
    return (coefficients, fitted.reshape(samples.shape[0], low_coef.shape[1]))


def solution(mesh):
    placed = (P(("rows", "rhs"), None), P(), P(), P(), P("rows", "rhs"))
    return jax.shard_map(
        body, mesh=mesh, in_specs=placed, out_specs=(P(), P(("rows", "rhs"), None)), check_vma=False
    )
```

```python
import functools
import math

import jax
import jax.numpy as jnp
from jax import lax
from jax.experimental import pallas as pl
from jax.experimental.pallas import tpu as pltpu
from jax.sharding import PartitionSpec as P

ridge = 0.05
MESH = pl.DeviceIdType.MESH
HIGHEST = lax.Precision.HIGHEST
VMEM = pl.BlockSpec(memory_space=pltpu.VMEM)
ANY = pl.BlockSpec(memory_space=pl.ANY)
HBM = pl.BlockSpec(memory_space=pltpu.HBM)
TILE = 128
SIN_TERMS = [3.141592580044735, -5.1677068789267455, 2.550031377285281, -0.598045174146624, 0.07722012899537994]


def split(x):
    high = x.astype(jnp.bfloat16)
    rest = x - high.astype(jnp.float32)
    middle = rest.astype(jnp.bfloat16)
    low = (rest - middle.astype(jnp.float32)).astype(jnp.bfloat16)
    return high, middle, low


def pick(table_ref, seed_ref, phase_ref):
    turn = jnp.float32(1.0 / (2.0 * math.pi))
    depth, length = table_ref.shape
    size = seed_ref.shape[1]
    tile = min(length, 512)
    stack = jnp.concatenate(split(table_ref[...] * turn), axis=0)
    row = lax.broadcasted_iota(jnp.int32, (tile, size), 0)
    found = jnp.zeros((3 * depth, size), jnp.float32)
    for k in range(0, length, tile):
        chosen = jnp.where(row == seed_ref[...] - k, 1.0, 0.0).astype(jnp.bfloat16)
        found += jnp.dot(stack[:, k : k + tile], chosen, preferred_element_type=jnp.float32)
    high, middle, low = (found[i * depth : (i + 1) * depth] for i in range(3))
    shift = [t.astype(jnp.float32) for t in split(phase_ref[...] * turn)]
    shift = jnp.concatenate(shift + [jnp.zeros((depth - 3, size), jnp.float32)], axis=0)
    full = jnp.concatenate([high, middle, high, middle, low, high, shift], axis=0)
    return full.T.astype(jnp.bfloat16)


def features(x, f):
    high, middle, low = split(x)
    ones = jnp.ones(x.shape, jnp.bfloat16)
    rows = jnp.concatenate([high, high, middle, middle, high, low, ones], axis=0)
    turns = jnp.dot(f, rows, preferred_element_type=jnp.float32)
    r = turns - jnp.round(turns)
    u = r * r
    scale = math.sqrt(2.0 * math.sqrt(2.0))
    s = u * (SIN_TERMS[-1] * scale) + SIN_TERMS[-2] * scale
    for term in reversed(SIN_TERMS[:-2]):
        s = s * u + term * scale
    s = s * r
    return (math.sqrt(2.0) - s * s).astype(jnp.bfloat16)


def exchange(R, Z, count, w_ref, got, out, sems):
    send, recv, zsend, zrecv, psend, precv, csend, crecv = sems
    r, z = lax.axis_index("rows"), lax.axis_index("rhs")
    core, spot, half = lax.rem(r, 2), r // 2, R // 2

    def copy(src, dst, out_sem, in_sem, d, peer):
        return pltpu.make_async_remote_copy(
            src_ref=src,
            dst_ref=dst,
            send_sem=out_sem.at[d],
            recv_sem=in_sem.at[d],
            device_id=peer,
            device_id_type=MESH,
        )

    def scatter(d):
        peer = lax.rem(r + d, R)
        return copy(w_ref.at[peer], got.at[d], send, recv, d, {"rows": peer})

    def along(d):
        mine = out.at[r, z]
        return copy(mine, mine, zsend, zrecv, d, {"rhs": lax.rem(z + d, Z)})

    def across(d):
        peer = lax.rem(spot + d, half) * 2 + core
        return copy(out.at[r], out.at[r], psend, precv, d, {"rows": peer})

    def aside(d):
        where = out.at[lax.rem(spot - d + half, half) * 2 + core]
        return copy(where, where, csend, crecv, d, {"rows": r + 1 - 2 * core})

    def first():
        for d in range(1, R):
            scatter(d).start()

    def second():
        total = w_ref[r]
        for d in range(1, R):
            scatter(d).wait()
            total = total + got[d]
        out[r, z] = total * (1.0 / count)
        for d in range(1, Z):
            along(d).start()

    def third():
        for d in range(1, Z):
            along(d).wait()
        for d in range(1, half):
            across(d).start()
        aside(0).start()

    def fourth():
        for d in range(1, half):
            across(d).wait()
            aside(d).start()

    def last():
        for d in range(half):
            aside(d).wait()

    return first, second, third, fourth, last


def sweep(a, base):
    shape = a[0].shape
    lane = lax.broadcasted_iota(jnp.int32, shape, 1)
    sub = lax.broadcasted_iota(jnp.int32, shape, 0)

    def across(v, j):
        return jnp.broadcast_to(v[:, j : j + 1], shape)

    def down(v, i):
        return jnp.broadcast_to(v[i : i + 1, :], shape)

    for g in range(len(a)):
        k = base + 8 * g
        c = [0.0 - across(a[g], k + j) for j in range(8)]
        far = [[across(v, k + j) for j in range(8)] if i != g else None for i, v in enumerate(a)]
        inside = jnp.logical_and(lane >= k, lane < k + 8)
        rows = jnp.where(inside, jnp.where(lane == sub + k, 1.0, 0.0), a[g])
        for s in range(0, 8, 2):
            p, q, r = down(c[s], s), down(c[s + 1], s), down(c[s + 1], s + 1)
            scale = 1.0 / (p * r - q * q)
            pair = jnp.logical_and(sub >= s, sub < s + 2)
            l0 = jnp.where(pair, jnp.where(sub == s, 1.0, 0.0), c[s])
            l1 = jnp.where(pair, jnp.where(sub == s, 0.0, 1.0), c[s + 1])

            def step(v):
                v0, v1 = down(v, s), down(v, s + 1)
                u0, u1 = r * v0 - q * v1, p * v1 - q * v0
                return jnp.where(pair, 0.0, v) - scale * (l0 * u0 + l1 * u1)

            rows = step(rows)
            for j in range(s + 2, 8):
                c[j] = step(c[j])
        w = [down(rows, i) for i in range(8)]
        for i in range(len(a)):
            if i == g:
                continue
            f = [far[i][j] * w[j] for j in range(8)]
            total = ((f[0] + f[1]) + (f[2] + f[3])) + ((f[4] + f[5]) + (f[6] + f[7]))
            a[i] = jnp.where(inside, 0.0, a[i]) - total
        a[g] = rows
    return a


def invert_block(ref, dst):
    half = TILE // 2
    groups = half // 8
    dot = functools.partial(jnp.dot, precision=HIGHEST, preferred_element_type=jnp.float32)
    left = lax.broadcasted_iota(jnp.int32, (half, TILE), 1) < half
    top = sweep([ref[8 * i : 8 * i + 8, :] for i in range(groups)], 0)
    for i in range(groups):
        dst[8 * i : 8 * i + 8, :] = top[i]
    lower = ref[half:, :]
    lower = jnp.where(left, 0.0, lower) - dot(lower[:, :half], dst[:half, :])
    low = sweep([lower[8 * i : 8 * i + 8, :] for i in range(groups)], half)
    for i in range(groups):
        dst[half + 8 * i : half + 8 * i + 8, :] = low[i]
    upper = dst[:half, :]
    dst[:half, :] = jnp.where(left, upper, 0.0) - dot(upper[:, half:], dst[half:, :])


def fused_kernel(
    R, Z, parts, count, x_hbm, table_hbm, seed_hbm, phase_hbm, t_hbm, coef_ref, low_ref, own,
    xs, table_ref, seed_ref, phase_ref, t_ref, f_ref, turned, acc, w, got, out, v, vgot, vout,
    gram, upper, lower, right, inverse, inner, send, recv, local, *rest
):
    phis, sems = rest[:parts], rest[parts:]
    r, z = lax.axis_index("rows"), lax.axis_index("rhs")
    size, panel = acc.shape
    chunk = x_hbm.shape[1] // parts
    blocks = size // TILE
    wanted = [(seed_hbm, seed_ref), (phase_hbm, phase_ref), (table_hbm, table_ref)]
    wanted += [(x_hbm.at[:, i * chunk : (i + 1) * chunk], xs.at[z, i]) for i in range(parts)]
    wanted += [(t_hbm, t_ref)]
    loads = [pltpu.make_async_copy(*pair, local.at[i]) for i, pair in enumerate(wanted)]
    for load in loads:
        load.start()
    barrier = pltpu.get_barrier_semaphore()
    for d in range(1, R):
        pl.semaphore_signal(
            barrier, inc=1, device_id={"rows": lax.rem(r + d, R)}, device_id_type=MESH
        )
    for d in range(1, Z):
        pl.semaphore_signal(
            barrier, inc=1, device_id={"rhs": lax.rem(z + d, Z)}, device_id_type=MESH
        )
    pl.semaphore_wait(barrier, R + Z - 2)

    def moving(q, way):
        block, part = z - way * (q // parts), lax.rem(q, parts)
        if isinstance(q, int):
            source = x_hbm.at[:, q * chunk : (q + 1) * chunk]
        else:
            source = xs.at[block, part]
        return pltpu.make_async_remote_copy(
            src_ref=source,
            dst_ref=xs.at[block, part],
            send_sem=send.at[(way + 1) // 2, q],
            recv_sem=recv.at[(way + 1) // 2, q],
            device_id={"rhs": z + way},
            device_id_type=MESH,
        )

    def arriving(q, way):
        block, part = z - way * (q // parts + 1), lax.rem(q, parts)
        return pltpu.make_async_remote_copy(
            src_ref=xs.at[block, part],
            dst_ref=xs.at[block, part],
            send_sem=send.at[(way + 1) // 2, q],
            recv_sem=recv.at[(way + 1) // 2, q],
            device_id={"rhs": z - way},
            device_id_type=MESH,
        )

    def inside(p):
        return jnp.logical_and(p >= 0, p < Z)

    for q in range(parts):
        for way in (1, -1):
            pl.when(inside(z + way))(lambda: moving(q, way).start())
    for load in loads[:-1]:
        load.wait()
    f_ref[...] = pick(table_ref, seed_ref, phase_ref)
    acc[...] = jnp.zeros_like(acc)
    near = jnp.minimum(z, Z - 1 - z)

    @pl.loop(0, Z)
    def _(d):
        for part in range(parts):
            q = (d - 1) * parts + part
            for way in (1, -1):

                @pl.when(jnp.logical_and(d > 0, inside(z - way * d)))
                def _():
                    arriving(q, way).wait_recv()
                    pl.when(inside(z + way))(lambda: moving(q + parts, way).start())

        step = (d + 1) // 2
        both = jnp.where(d % 2 == 1, z - step, z + step)
        single = jnp.where(z < Z - 1 - z, z + d - near, z - d + near)
        block = jnp.where(d <= 2 * near, both, single)
        for part, phi in enumerate(phis):
            phi[block] = features(xs[block, part], f_ref[...])
            mine = phi[block, pl.ds(pl.multiple_of(z * panel, panel), panel), :]
            turned[part] = mine.T
            acc[...] += jnp.dot(phi[block], turned[part], preferred_element_type=jnp.float32)

    @pl.loop(0, Z * parts)
    def _(q):
        for way in (1, -1):
            sent = jnp.logical_and(inside(z + way), inside(z - way * (q // parts)))
            pl.when(sent)(lambda: moving(q, way).wait_send())

    stages = [
        exchange(R, Z, count, w.at[c], got.at[c], out.at[c], [s.at[c] for s in sems[:8]])
        for c in range(blocks)
    ]
    rows = TILE // R
    for c in range(blocks):
        for i in range(R):
            at = c * TILE + i * rows
            w[c, i] = acc[at : at + rows, :]
        stages[c][0]()
    loads[-1].wait()
    acc[...] = jnp.zeros_like(acc)

    def cross(low, high):
        @pl.loop(low, high)
        def _(block):
            for part, phi in enumerate(phis):
                here = pl.multiple_of((block * parts + part) * chunk, chunk)
                acc[...] += jnp.dot(
                    phi[block], t_ref[pl.ds(here, chunk), :], preferred_element_type=jnp.float32
                )

    def keep(part):
        own[part] = phis[part][z].T

    def spread(source, dest, base, height):
        for i in range(R):
            for j in range(Z):
                top = base + i * height
                dest[top : top + height, j * panel : (j + 1) * panel] = source[i, j]

    cross(0, Z // 2)
    stages[0][1]()
    cross(Z // 2, Z)
    for c in range(1, blocks):
        stages[c][1]()
    stages[0][2]()
    high = size // R
    for i in range(R):
        v[i] = acc[i * high : (i + 1) * high, :]
    last = exchange(R, Z, count, v, vgot, vout, sems[8:])
    last[0]()
    for c in range(1, blocks):
        stages[c][2]()
    for part in range(parts):
        keep(part)
    stages[0][3]()
    for c in range(1, blocks):
        stages[c][3]()
    last[1]()
    stages[0][4]()
    spread(out.at[0], gram, 0, rows)
    row = lax.broadcasted_iota(jnp.int32, (TILE, TILE), 0)
    col = lax.broadcasted_iota(jnp.int32, (TILE, TILE), 1)
    eye = jnp.where(row == col, jnp.float32(ridge), 0.0)
    dot = functools.partial(jnp.dot, precision=HIGHEST, preferred_element_type=jnp.float32)

    def at(i):
        return slice(i * TILE, (i + 1) * TILE)

    @pl.loop(0, blocks)
    def _(k):
        mine = pl.ds(pl.multiple_of(k * TILE, TILE), TILE)

        @pl.loop(0, k)
        def _(i):
            above = pl.ds(pl.multiple_of(i * TILE, TILE), TILE)
            left = upper[above, mine].T
            lower[mine, above] = left
            gram[mine, :] -= dot(left, gram[above, :])

        upper[mine, :] = gram[mine, :]
        inner[...] = gram[mine, mine] + eye
        invert_block(inner, inverse.at[k])
        gram[mine, :] = dot(inverse[k], upper[mine, :])
        for c in range(1, blocks):

            @pl.when(k == c - 1)
            def _():
                stages[c][4]()
                spread(out.at[c], gram, c * TILE, rows)

        for i, stage in enumerate(last[2:]):
            pl.when(k == min(i, blocks - 1))(stage)

    spread(vout, right, 0, high)
    for k in range(blocks):
        value = right[at(k), :]
        if k:
            value -= dot(lower[at(k), : k * TILE], right[: k * TILE, :])
        right[at(k), :] = dot(inverse[k], value)
    for k in reversed(range(blocks)):
        value = right[at(k), :]
        if k + 1 < blocks:
            value -= dot(gram[at(k), (k + 1) * TILE :], coef_ref[(k + 1) * TILE :, :])
        coef_ref[at(k), :] = value
        low_ref[at(k), :] = value.astype(jnp.bfloat16)


def fused(x, table, seeds, phases, targets):
    R, Z = lax.axis_size("rows"), lax.axis_size("rhs")
    depth, length = x.shape
    size = seeds.shape[1]
    panel = targets.shape[1]
    columns = Z * panel
    chunk = min(length, 512)
    parts = length // chunk
    blocks = size // TILE
    rows, high = TILE // R, size // R
    sems = pltpu.SemaphoreType.DMA
    f32, bf16 = jnp.float32, jnp.bfloat16
    place = lambda v: pltpu.with_memory_space_constraint(v, pltpu.HBM)
    return pl.pallas_call(
        functools.partial(fused_kernel, R, Z, parts, length * R * Z),
        out_shape=[
            pltpu.VMEM((size, columns), f32),
            pltpu.VMEM((size, columns), bf16),
            pltpu.VMEM((parts, chunk, size), bf16),
        ],
        in_specs=[HBM] * 5,
        out_specs=[VMEM, VMEM, VMEM],
        scratch_shapes=[
            pltpu.VMEM((Z, parts, depth, chunk), f32),
            pltpu.VMEM(table.shape, f32),
            pltpu.VMEM(seeds.shape, jnp.int32),
            pltpu.VMEM(phases.shape, f32),
            pltpu.VMEM(targets.shape, targets.dtype),
            pltpu.VMEM((size, 7 * depth), bf16),
            pltpu.VMEM((parts, chunk, panel), bf16),
            pltpu.VMEM((size, panel), f32),
            pltpu.VMEM((blocks, R, rows, panel), f32),
            pltpu.VMEM((blocks, R, rows, panel), f32),
            pltpu.VMEM((blocks, R, Z, rows, panel), f32),
            pltpu.VMEM((R, high, panel), f32),
            pltpu.VMEM((R, high, panel), f32),
            pltpu.VMEM((R, Z, high, panel), f32),
            pltpu.VMEM((size, size), f32),
            pltpu.VMEM((size, size), f32),
            pltpu.VMEM((size, size), f32),
            pltpu.VMEM((size, columns), f32),
            pltpu.VMEM((blocks, TILE, TILE), f32),
            pltpu.VMEM((TILE, TILE), f32),
            sems((2, Z * parts)),
            sems((2, Z * parts)),
            sems((4 + parts,)),
        ]
        + [pltpu.VMEM((Z, size, chunk), bf16)] * parts
        + [sems((blocks, R))] * 2 + [sems((blocks, Z))] * 2 + [sems((blocks, R))] * 4
        + [sems((R,))] * 2 + [sems((Z,))] * 2 + [sems((R,))] * 4,
        compiler_params=pltpu.CompilerParams(collective_id=0, has_side_effects=True, vmem_limit_bytes=40 << 20),
    )(*map(place, (x, table, seeds, phases, targets)))


def fit_kernel(own_ref, low_ref, coef_ref, coef_out, fitted_out, fitted, sems):
    parts, chunk = own_ref.shape[:2]
    copies = [pltpu.make_async_copy(coef_ref, coef_out, sems.at[0])]
    copies[0].start()
    half = chunk // 2
    for part in range(parts):
        for side in range(2):
            rows = slice(side * half, (side + 1) * half)
            fitted[part, rows, :] = jnp.dot(
                own_ref[part, rows, :], low_ref[...], preferred_element_type=jnp.float32
            )
            i = 2 * part + side
            copies.append(
                pltpu.make_async_copy(
                    fitted.at[part, rows], fitted_out.at[part, rows], sems.at[1 + i]
                )
            )
            copies[-1].start()
    for copy in copies:
        copy.wait()


def fit(own, low, coef):
    parts, chunk, size = own.shape
    columns = low.shape[1]
    shape = (parts, chunk, columns)
    return pl.pallas_call(
        fit_kernel,
        in_specs=[VMEM, VMEM, VMEM],
        out_specs=[ANY, ANY],
        out_shape=[
            jax.ShapeDtypeStruct((size, columns), jnp.float32),
            jax.ShapeDtypeStruct(shape, jnp.float32),
        ],
        scratch_shapes=[
            pltpu.VMEM(shape, jnp.float32),
            pltpu.SemaphoreType.DMA((1 + 2 * parts,)),
        ],
        compiler_params=pltpu.CompilerParams(vmem_limit_bytes=16 << 20),
    )(own, low, coef)


def body(samples, freq_table, feature_seeds, phases, treatment_features):
    seeds, shifts = feature_seeds.reshape(1, -1), phases.reshape(1, -1)
    coef, low_coef, own = fused(samples.T, freq_table.T, seeds, shifts, treatment_features)
    coefficients, fitted = fit(own, low_coef, coef)
    return (coefficients, fitted.reshape(samples.shape[0], low_coef.shape[1]))


def solution(mesh):
    placed = (P(("rows", "rhs"), None), P(), P(), P(), P("rows", "rhs"))
    return jax.shard_map(
        body, mesh=mesh, in_specs=placed, out_specs=(P(), P(("rows", "rhs"), None)), check_vma=False
    )
```

```python
import functools
import math

import jax
import jax.numpy as jnp
from jax import lax
from jax.experimental import pallas as pl
from jax.experimental.pallas import tpu as pltpu
from jax.sharding import PartitionSpec as P

ridge = 0.05
MESH = pl.DeviceIdType.MESH
HIGHEST = lax.Precision.HIGHEST
VMEM = pl.BlockSpec(memory_space=pltpu.VMEM)
ANY = pl.BlockSpec(memory_space=pl.ANY)
HBM = pl.BlockSpec(memory_space=pltpu.HBM)
TILE = 128
SIN_TERMS = [3.141592580044735, -5.1677068789267455, 2.550031377285281, -0.598045174146624, 0.07722012899537994]


def split(x):
    high = x.astype(jnp.bfloat16)
    rest = x - high.astype(jnp.float32)
    middle = rest.astype(jnp.bfloat16)
    low = (rest - middle.astype(jnp.float32)).astype(jnp.bfloat16)
    return high, middle, low


def pick(table_ref, seed_ref, phase_ref):
    turn = jnp.float32(1.0 / (2.0 * math.pi))
    depth, length = table_ref.shape
    size = seed_ref.shape[1]
    tile = min(length, 512)
    stack = jnp.concatenate(split(table_ref[...] * turn), axis=0)
    row = lax.broadcasted_iota(jnp.int32, (tile, size), 0)
    found = jnp.zeros((3 * depth, size), jnp.float32)
    for k in range(0, length, tile):
        chosen = jnp.where(row == seed_ref[...] - k, 1.0, 0.0).astype(jnp.bfloat16)
        found += jnp.dot(stack[:, k : k + tile], chosen, preferred_element_type=jnp.float32)
    high, middle, low = (found[i * depth : (i + 1) * depth] for i in range(3))
    shift = [t.astype(jnp.float32) for t in split(phase_ref[...] * turn)]
    shift = jnp.concatenate(shift + [jnp.zeros((depth - 3, size), jnp.float32)], axis=0)
    full = jnp.concatenate([high, middle, high, middle, low, high, shift], axis=0)
    return full.T.astype(jnp.bfloat16)


def features(x, f):
    high, middle, low = split(x)
    ones = jnp.ones(x.shape, jnp.bfloat16)
    rows = jnp.concatenate([high, high, middle, middle, high, low, ones], axis=0)
    turns = jnp.dot(f, rows, preferred_element_type=jnp.float32)
    r = turns - jnp.round(turns)
    u = r * r
    scale = math.sqrt(2.0 * math.sqrt(2.0))
    s = u * (SIN_TERMS[-1] * scale) + SIN_TERMS[-2] * scale
    for term in reversed(SIN_TERMS[:-2]):
        s = s * u + term * scale
    s = s * r
    return (math.sqrt(2.0) - s * s).astype(jnp.bfloat16)


def exchange(R, Z, low, count, w_ref, got, out, sems):
    send, recv, zsend, zrecv, psend, precv, csend, crecv = sems
    r, z = lax.axis_index("rows"), lax.axis_index("rhs")
    core, spot, half = lax.rem(r, 2), r // 2, R // 2

    def holds(column):
        return (lambda f: f()) if low == 0 else pl.when(column >= low)

    def copy(src, dst, out_sem, in_sem, d, peer):
        return pltpu.make_async_remote_copy(
            src_ref=src,
            dst_ref=dst,
            send_sem=out_sem.at[d],
            recv_sem=in_sem.at[d],
            device_id=peer,
            device_id_type=MESH,
        )

    def scatter(d):
        peer = lax.rem(r + d, R)
        return copy(w_ref.at[peer], got.at[d], send, recv, d, {"rows": peer})

    def along(d):
        mine = out.at[r, z]
        return copy(mine, mine, zsend, zrecv, d, {"rhs": lax.rem(z + d, Z)})

    def across(d):
        peer = lax.rem(spot + d, half) * 2 + core
        where = out.at[r, low:]
        return copy(where, where, psend, precv, d, {"rows": peer})

    def aside(d):
        where = out.at[lax.rem(spot - d + half, half) * 2 + core, low:]
        return copy(where, where, csend, crecv, d, {"rows": r + 1 - 2 * core})

    def first():
        @holds(z)
        def _():
            for d in range(1, R):
                scatter(d).start()

    def second():
        @holds(z)
        def _():
            total = w_ref[r]
            for d in range(1, R):
                scatter(d).wait()
                total = total + got[d]
            out[r, z] = total * (1.0 / count)
            for d in range(1, Z):
                along(d).start()

    def third():
        for d in range(1, Z):
            holds(lax.rem(z - d + Z, Z))(along(d).wait_recv)
        for d in range(1, half):
            across(d).start()
        aside(0).start()

    def fourth():
        for d in range(1, half):
            across(d).wait()
            aside(d).start()

    def last():
        for d in range(half):
            aside(d).wait()

        @holds(z)
        def _():
            for d in range(1, Z):
                along(d).wait_send()

    return first, second, third, fourth, last


def sweep(a, base):
    shape = a[0].shape
    lane = lax.broadcasted_iota(jnp.int32, shape, 1)
    sub = lax.broadcasted_iota(jnp.int32, shape, 0)

    def across(v, j):
        return jnp.broadcast_to(v[:, j : j + 1], shape)

    def down(v, i):
        return jnp.broadcast_to(v[i : i + 1, :], shape)

    for g in range(len(a)):
        k = base + 8 * g
        c = [0.0 - across(a[g], k + j) for j in range(8)]
        far = [[across(v, k + j) for j in range(8)] if i != g else None for i, v in enumerate(a)]
        inside = jnp.logical_and(lane >= k, lane < k + 8)
        rows = jnp.where(inside, jnp.where(lane == sub + k, 1.0, 0.0), a[g])
        for s in range(0, 8, 2):
            p, q, r = down(c[s], s), down(c[s + 1], s), down(c[s + 1], s + 1)
            scale = 1.0 / (p * r - q * q)
            pair = jnp.logical_and(sub >= s, sub < s + 2)
            l0 = jnp.where(pair, jnp.where(sub == s, 1.0, 0.0), c[s])
            l1 = jnp.where(pair, jnp.where(sub == s, 0.0, 1.0), c[s + 1])

            def step(v):
                v0, v1 = down(v, s), down(v, s + 1)
                u0, u1 = r * v0 - q * v1, p * v1 - q * v0
                return jnp.where(pair, 0.0, v) - scale * (l0 * u0 + l1 * u1)

            rows = step(rows)
            for j in range(s + 2, 8):
                c[j] = step(c[j])
        w = [down(rows, i) for i in range(8)]
        for i in range(len(a)):
            if i == g:
                continue
            f = [far[i][j] * w[j] for j in range(8)]
            total = ((f[0] + f[1]) + (f[2] + f[3])) + ((f[4] + f[5]) + (f[6] + f[7]))
            a[i] = jnp.where(inside, 0.0, a[i]) - total
        a[g] = rows
    return a


def invert_block(ref, dst):
    half = TILE // 2
    groups = half // 8
    dot = functools.partial(jnp.dot, precision=HIGHEST, preferred_element_type=jnp.float32)
    left = lax.broadcasted_iota(jnp.int32, (half, TILE), 1) < half
    top = sweep([ref[8 * i : 8 * i + 8, :] for i in range(groups)], 0)
    for i in range(groups):
        dst[8 * i : 8 * i + 8, :] = top[i]
    lower = ref[half:, :]
    lower = jnp.where(left, 0.0, lower) - dot(lower[:, :half], dst[:half, :])
    low = sweep([lower[8 * i : 8 * i + 8, :] for i in range(groups)], half)
    for i in range(groups):
        dst[half + 8 * i : half + 8 * i + 8, :] = low[i]
    upper = dst[:half, :]
    dst[:half, :] = jnp.where(left, upper, 0.0) - dot(upper[:, half:], dst[half:, :])


def fused_kernel(
    R, Z, parts, count, x_hbm, table_hbm, seed_hbm, phase_hbm, t_hbm, coef_ref, low_ref, own,
    xs, table_ref, seed_ref, phase_ref, t_ref, f_ref, turned, acc, w, got, out, v, vgot, vout,
    gram, upper, lower, right, inverse, inner, send, recv, local, *rest
):
    phis, sems = rest[:parts], rest[parts:]
    r, z = lax.axis_index("rows"), lax.axis_index("rhs")
    size, panel = acc.shape[0], t_ref.shape[1]
    chunk = x_hbm.shape[1] // parts
    blocks = size // TILE
    wanted = [(seed_hbm, seed_ref), (phase_hbm, phase_ref), (table_hbm, table_ref)]
    wanted += [(x_hbm.at[:, i * chunk : (i + 1) * chunk], xs.at[z, i]) for i in range(parts)]
    wanted += [(t_hbm, t_ref)]
    loads = [pltpu.make_async_copy(*pair, local.at[i]) for i, pair in enumerate(wanted)]
    for load in loads:
        load.start()
    barrier = pltpu.get_barrier_semaphore()
    for d in range(1, R):
        pl.semaphore_signal(
            barrier, inc=1, device_id={"rows": lax.rem(r + d, R)}, device_id_type=MESH
        )
    for d in range(1, Z):
        pl.semaphore_signal(
            barrier, inc=1, device_id={"rhs": lax.rem(z + d, Z)}, device_id_type=MESH
        )
    pl.semaphore_wait(barrier, R + Z - 2)

    def moving(q, way):
        block, part = z - way * (q // parts), lax.rem(q, parts)
        if isinstance(q, int):
            source = x_hbm.at[:, q * chunk : (q + 1) * chunk]
        else:
            source = xs.at[block, part]
        return pltpu.make_async_remote_copy(
            src_ref=source,
            dst_ref=xs.at[block, part],
            send_sem=send.at[(way + 1) // 2, q],
            recv_sem=recv.at[(way + 1) // 2, q],
            device_id={"rhs": z + way},
            device_id_type=MESH,
        )

    def arriving(q, way):
        block, part = z - way * (q // parts + 1), lax.rem(q, parts)
        return pltpu.make_async_remote_copy(
            src_ref=xs.at[block, part],
            dst_ref=xs.at[block, part],
            send_sem=send.at[(way + 1) // 2, q],
            recv_sem=recv.at[(way + 1) // 2, q],
            device_id={"rhs": z - way},
            device_id_type=MESH,
        )

    def inside(p):
        return jnp.logical_and(p >= 0, p < Z)

    for q in range(parts):
        for way in (1, -1):
            pl.when(inside(z + way))(lambda: moving(q, way).start())
    for load in loads:
        load.wait()
    f_ref[...] = pick(table_ref, seed_ref, phase_ref)
    acc[...] = jnp.zeros_like(acc)
    near = jnp.minimum(z, Z - 1 - z)

    @pl.loop(0, Z)
    def _(d):
        for part in range(parts):
            q = (d - 1) * parts + part
            for way in (1, -1):

                @pl.when(jnp.logical_and(d > 0, inside(z - way * d)))
                def _():
                    arriving(q, way).wait_recv()
                    pl.when(inside(z + way))(lambda: moving(q + parts, way).start())

        step = (d + 1) // 2
        both = jnp.where(d % 2 == 1, z - step, z + step)
        single = jnp.where(z < Z - 1 - z, z + d - near, z - d + near)
        block = jnp.where(d <= 2 * near, both, single)
        for part, phi in enumerate(phis):
            phi[block] = features(xs[block, part], f_ref[...])
            mine = phi[block, pl.ds(pl.multiple_of(z * panel, panel), panel), :]
            turned[part, :, :panel] = mine.T
            here = pl.multiple_of((block * parts + part) * chunk, chunk)
            turned[part, :, panel:] = t_ref[pl.ds(here, chunk), :]
            acc[...] += jnp.dot(phi[block], turned[part], preferred_element_type=jnp.float32)

    @pl.loop(0, Z * parts)
    def _(q):
        for way in (1, -1):
            sent = jnp.logical_and(inside(z + way), inside(z - way * (q // parts)))
            pl.when(sent)(lambda: moving(q, way).wait_send())

    stages = [
        exchange(
            R, Z, c * TILE // panel, count, w.at[c], got.at[c], out.at[c],
            [s.at[c] for s in sems[:8]],
        )
        for c in range(blocks)
    ]
    rows = TILE // R
    for c in range(blocks):
        for i in range(R):
            at = c * TILE + i * rows
            w[c, i] = acc[at : at + rows, :panel]
        stages[c][0]()
    high = size // R
    for i in range(R):
        v[i] = acc[i * high : (i + 1) * high, panel:]
    last = exchange(R, Z, 0, count, v, vgot, vout, sems[8:])
    last[0]()

    def keep(part):
        own[part] = phis[part][z].T

    def spread(source, dest, base, height, first=0):
        for i in range(R):
            for j in range(first, Z):
                top = base + i * height
                dest[top : top + height, j * panel : (j + 1) * panel] = source[i, j]

    for step in (1, 2):
        for c in range(blocks):
            stages[c][step]()
    for part in range(parts):
        keep(part)
    stages[0][3]()
    last[1]()
    for c in range(1, blocks):
        stages[c][3]()
    stages[0][4]()
    spread(out.at[0], gram, 0, rows)
    row = lax.broadcasted_iota(jnp.int32, (TILE, TILE), 0)
    col = lax.broadcasted_iota(jnp.int32, (TILE, TILE), 1)
    eye = jnp.where(row == col, jnp.float32(ridge), 0.0)
    dot = functools.partial(jnp.dot, precision=HIGHEST, preferred_element_type=jnp.float32)

    def at(i):
        return slice(i * TILE, (i + 1) * TILE)

    @pl.loop(0, blocks)
    def _(k):
        mine = pl.ds(pl.multiple_of(k * TILE, TILE), TILE)

        @pl.loop(0, k)
        def _(i):
            above = pl.ds(pl.multiple_of(i * TILE, TILE), TILE)
            left = upper[above, mine].T
            lower[mine, above] = left
            gram[mine, :] -= dot(left, gram[above, :])

        upper[mine, :] = gram[mine, :]
        inner[...] = gram[mine, mine] + eye
        invert_block(inner, inverse.at[k])
        gram[mine, :] = dot(inverse[k], upper[mine, :])
        for c in range(1, blocks):

            @pl.when(k == c - 1)
            def _():
                stages[c][4]()
                spread(out.at[c], gram, c * TILE, rows, c * TILE // panel)

        for i, stage in ((0, last[2]), (2, last[3]), (3, last[4])):
            pl.when(k == min(i, blocks - 1))(stage)

    spread(vout, right, 0, high)
    for k in range(blocks):
        value = right[at(k), :]
        if k:
            value -= dot(lower[at(k), : k * TILE], right[: k * TILE, :])
        right[at(k), :] = dot(inverse[k], value)
    for k in reversed(range(blocks)):
        value = right[at(k), :]
        if k + 1 < blocks:
            value -= dot(gram[at(k), (k + 1) * TILE :], coef_ref[(k + 1) * TILE :, :])
        coef_ref[at(k), :] = value
        low_ref[at(k), :] = value.astype(jnp.bfloat16)


def fused(x, table, seeds, phases, targets):
    R, Z = lax.axis_size("rows"), lax.axis_size("rhs")
    depth, length = x.shape
    size = seeds.shape[1]
    panel = targets.shape[1]
    columns = Z * panel
    chunk = min(length, 512)
    parts = length // chunk
    blocks = size // TILE
    rows, high = TILE // R, size // R
    sems = pltpu.SemaphoreType.DMA
    f32, bf16 = jnp.float32, jnp.bfloat16
    place = lambda v: pltpu.with_memory_space_constraint(v, pltpu.HBM)
    return pl.pallas_call(
        functools.partial(fused_kernel, R, Z, parts, length * R * Z),
        out_shape=[
            pltpu.VMEM((size, columns), f32),
            pltpu.VMEM((size, columns), bf16),
            pltpu.VMEM((parts, chunk, size), bf16),
        ],
        in_specs=[HBM] * 5,
        out_specs=[VMEM, VMEM, VMEM],
        scratch_shapes=[
            pltpu.VMEM((Z, parts, depth, chunk), f32),
            pltpu.VMEM(table.shape, f32),
            pltpu.VMEM(seeds.shape, jnp.int32),
            pltpu.VMEM(phases.shape, f32),
            pltpu.VMEM(targets.shape, targets.dtype),
            pltpu.VMEM((size, 7 * depth), bf16),
            pltpu.VMEM((parts, chunk, 2 * panel), bf16),
            pltpu.VMEM((size, 2 * panel), f32),
            pltpu.VMEM((blocks, R, rows, panel), f32),
            pltpu.VMEM((blocks, R, rows, panel), f32),
            pltpu.VMEM((blocks, R, Z, rows, panel), f32),
            pltpu.VMEM((R, high, panel), f32),
            pltpu.VMEM((R, high, panel), f32),
            pltpu.VMEM((R, Z, high, panel), f32),
            pltpu.VMEM((size, size), f32),
            pltpu.VMEM((size, size), f32),
            pltpu.VMEM((size, size), f32),
            pltpu.VMEM((size, columns), f32),
            pltpu.VMEM((blocks, TILE, TILE), f32),
            pltpu.VMEM((TILE, TILE), f32),
            sems((2, Z * parts)),
            sems((2, Z * parts)),
            sems((4 + parts,)),
        ]
        + [pltpu.VMEM((Z, size, chunk), bf16)] * parts
        + [sems((blocks, R))] * 2 + [sems((blocks, Z))] * 2 + [sems((blocks, R))] * 4
        + [sems((R,))] * 2 + [sems((Z,))] * 2 + [sems((R,))] * 4,
        compiler_params=pltpu.CompilerParams(collective_id=0, has_side_effects=True, vmem_limit_bytes=40 << 20),
    )(*map(place, (x, table, seeds, phases, targets)))


def fit_kernel(own_ref, low_ref, coef_ref, coef_out, fitted_out, fitted, sems):
    parts, chunk = own_ref.shape[:2]
    copies = [pltpu.make_async_copy(coef_ref, coef_out, sems.at[0])]
    copies[0].start()
    half = chunk // 2
    for part in range(parts):
        for side in range(2):
            rows = slice(side * half, (side + 1) * half)
            fitted[part, rows, :] = jnp.dot(
                own_ref[part, rows, :], low_ref[...], preferred_element_type=jnp.float32
            )
            i = 2 * part + side
            copies.append(
                pltpu.make_async_copy(
                    fitted.at[part, rows], fitted_out.at[part, rows], sems.at[1 + i]
                )
            )
            copies[-1].start()
    for copy in copies:
        copy.wait()


def fit(own, low, coef):
    parts, chunk, size = own.shape
    columns = low.shape[1]
    shape = (parts, chunk, columns)
    return pl.pallas_call(
        fit_kernel,
        in_specs=[VMEM, VMEM, VMEM],
        out_specs=[ANY, ANY],
        out_shape=[
            jax.ShapeDtypeStruct((size, columns), jnp.float32),
            jax.ShapeDtypeStruct(shape, jnp.float32),
        ],
        scratch_shapes=[
            pltpu.VMEM(shape, jnp.float32),
            pltpu.SemaphoreType.DMA((1 + 2 * parts,)),
        ],
        compiler_params=pltpu.CompilerParams(vmem_limit_bytes=16 << 20),
    )(own, low, coef)


def body(samples, freq_table, feature_seeds, phases, treatment_features):
    seeds, shifts = feature_seeds.reshape(1, -1), phases.reshape(1, -1)
    coef, low_coef, own = fused(samples.T, freq_table.T, seeds, shifts, treatment_features)
    coefficients, fitted = fit(own, low_coef, coef)
    return (coefficients, fitted.reshape(samples.shape[0], low_coef.shape[1]))


def solution(mesh):
    placed = (P(("rows", "rhs"), None), P(), P(), P(), P("rows", "rhs"))
    return jax.shard_map(
        body, mesh=mesh, in_specs=placed, out_specs=(P(), P(("rows", "rhs"), None)), check_vma=False
    )
```

```python
import functools
import math

import jax
import jax.numpy as jnp
from jax import lax
from jax.experimental import pallas as pl
from jax.experimental.pallas import tpu as pltpu
from jax.sharding import PartitionSpec as P

ridge = 0.05
MESH = pl.DeviceIdType.MESH
HIGHEST = lax.Precision.HIGHEST
VMEM = pl.BlockSpec(memory_space=pltpu.VMEM)
ANY = pl.BlockSpec(memory_space=pl.ANY)
HBM = pl.BlockSpec(memory_space=pltpu.HBM)
TILE = 128
SIN_TERMS = [3.141592580044735, -5.1677068789267455, 2.550031377285281, -0.598045174146624, 0.07722012899537994]


def split(x):
    high = x.astype(jnp.bfloat16)
    rest = x - high.astype(jnp.float32)
    middle = rest.astype(jnp.bfloat16)
    low = (rest - middle.astype(jnp.float32)).astype(jnp.bfloat16)
    return high, middle, low


def exact(a, b):
    ah, am, al = split(a)
    bh, bm, bl = split(b)
    return jnp.dot(
        jnp.concatenate([am, al, am, ah, ah, ah], axis=1),
        jnp.concatenate([bm, bh, bh, bl, bm, bh], axis=0),
        preferred_element_type=jnp.float32,
    )


def pick(table_ref, seed_ref, phase_ref):
    turn = jnp.float32(1.0 / (2.0 * math.pi))
    depth, length = table_ref.shape
    size = seed_ref.shape[1]
    tile = min(length, 512)
    stack = jnp.concatenate(split(table_ref[...] * turn), axis=0)
    row = lax.broadcasted_iota(jnp.int32, (tile, size), 0)
    found = jnp.zeros((3 * depth, size), jnp.float32)
    for k in range(0, length, tile):
        chosen = jnp.where(row == seed_ref[...] - k, 1.0, 0.0).astype(jnp.bfloat16)
        found += jnp.dot(stack[:, k : k + tile], chosen, preferred_element_type=jnp.float32)
    high, middle, low = (found[i * depth : (i + 1) * depth] for i in range(3))
    shift = [t.astype(jnp.float32) for t in split(phase_ref[...] * turn)]
    shift = jnp.concatenate(shift + [jnp.zeros((depth - 3, size), jnp.float32)], axis=0)
    full = jnp.concatenate([high, middle, high, middle, low, high, shift], axis=0)
    return full.T.astype(jnp.bfloat16)


def features(x, f):
    high, middle, low = split(x)
    ones = jnp.ones(x.shape, jnp.bfloat16)
    rows = jnp.concatenate([high, high, middle, middle, high, low, ones], axis=0)
    turns = jnp.dot(f, rows, preferred_element_type=jnp.float32)
    r = turns - jnp.round(turns)
    u = r * r
    scale = math.sqrt(2.0 * math.sqrt(2.0))
    s = u * (SIN_TERMS[-1] * scale) + SIN_TERMS[-2] * scale
    for term in reversed(SIN_TERMS[:-2]):
        s = s * u + term * scale
    s = s * r
    return (math.sqrt(2.0) - s * s).astype(jnp.bfloat16)


def exchange(R, Z, low, count, w_ref, got, out, sems):
    send, recv, zsend, zrecv, psend, precv, csend, crecv = sems
    r, z = lax.axis_index("rows"), lax.axis_index("rhs")
    core, spot, half = lax.rem(r, 2), r // 2, R // 2

    def holds(column):
        return (lambda f: f()) if low == 0 else pl.when(column >= low)

    def copy(src, dst, out_sem, in_sem, d, peer):
        return pltpu.make_async_remote_copy(
            src_ref=src,
            dst_ref=dst,
            send_sem=out_sem.at[d],
            recv_sem=in_sem.at[d],
            device_id=peer,
            device_id_type=MESH,
        )

    def scatter(d):
        peer = lax.rem(r + d, R)
        return copy(w_ref.at[peer], got.at[d], send, recv, d, {"rows": peer})

    def along(d):
        mine = out.at[r, z]
        return copy(mine, mine, zsend, zrecv, d, {"rhs": lax.rem(z + d, Z)})

    def across(d):
        peer = lax.rem(spot + d, half) * 2 + core
        where = out.at[r, low:]
        return copy(where, where, psend, precv, d, {"rows": peer})

    def aside(d):
        where = out.at[lax.rem(spot - d + half, half) * 2 + core, low:]
        return copy(where, where, csend, crecv, d, {"rows": r + 1 - 2 * core})

    def first():
        @holds(z)
        def _():
            for d in range(1, R):
                scatter(d).start()

    def second():
        @holds(z)
        def _():
            total = w_ref[r]
            for d in range(1, R):
                scatter(d).wait()
                total = total + got[d]
            out[r, z] = total * (1.0 / count)
            for d in range(1, Z):
                along(d).start()

    def third():
        for d in range(1, Z):
            holds(lax.rem(z - d + Z, Z))(along(d).wait_recv)
        for d in range(1, half):
            across(d).start()
        aside(0).start()

    def fourth():
        for d in range(1, half):
            across(d).wait()
            aside(d).start()

    def last():
        for d in range(half):
            aside(d).wait()

        @holds(z)
        def _():
            for d in range(1, Z):
                along(d).wait_send()

    return first, second, third, fourth, last


def sweep(a, base):
    shape = a[0].shape
    lane = lax.broadcasted_iota(jnp.int32, shape, 1)
    sub = lax.broadcasted_iota(jnp.int32, shape, 0)

    def across(v, j):
        return jnp.broadcast_to(v[:, j : j + 1], shape)

    def down(v, i):
        return jnp.broadcast_to(v[i : i + 1, :], shape)

    for g in range(len(a)):
        k = base + 8 * g
        c = [0.0 - across(a[g], k + j) for j in range(8)]
        far = [[across(v, k + j) for j in range(8)] if i != g else None for i, v in enumerate(a)]
        inside = jnp.logical_and(lane >= k, lane < k + 8)
        rows = jnp.where(inside, jnp.where(lane == sub + k, 1.0, 0.0), a[g])
        for s in range(0, 8, 2):
            p, q, r = down(c[s], s), down(c[s + 1], s), down(c[s + 1], s + 1)
            scale = 1.0 / (p * r - q * q)
            pair = jnp.logical_and(sub >= s, sub < s + 2)
            l0 = jnp.where(pair, jnp.where(sub == s, 1.0, 0.0), c[s])
            l1 = jnp.where(pair, jnp.where(sub == s, 0.0, 1.0), c[s + 1])

            def step(v):
                v0, v1 = down(v, s), down(v, s + 1)
                u0, u1 = r * v0 - q * v1, p * v1 - q * v0
                return jnp.where(pair, 0.0, v) - scale * (l0 * u0 + l1 * u1)

            rows = step(rows)
            for j in range(s + 2, 8):
                c[j] = step(c[j])
        w = [down(rows, i) for i in range(8)]
        for i in range(len(a)):
            if i == g:
                continue
            f = [far[i][j] * w[j] for j in range(8)]
            total = ((f[0] + f[1]) + (f[2] + f[3])) + ((f[4] + f[5]) + (f[6] + f[7]))
            a[i] = jnp.where(inside, 0.0, a[i]) - total
        a[g] = rows
    return a


def invert_block(ref, dst):
    half = TILE // 2
    groups = half // 8
    dot = functools.partial(jnp.dot, precision=HIGHEST, preferred_element_type=jnp.float32)
    left = lax.broadcasted_iota(jnp.int32, (half, TILE), 1) < half
    top = sweep([ref[8 * i : 8 * i + 8, :] for i in range(groups)], 0)
    for i in range(groups):
        dst[8 * i : 8 * i + 8, :] = top[i]
    lower = ref[half:, :]
    lower = jnp.where(left, 0.0, lower) - dot(lower[:, :half], dst[:half, :])
    low = sweep([lower[8 * i : 8 * i + 8, :] for i in range(groups)], half)
    for i in range(groups):
        dst[half + 8 * i : half + 8 * i + 8, :] = low[i]
    upper = dst[:half, :]
    dst[:half, :] = jnp.where(left, upper, 0.0) - dot(upper[:, half:], dst[half:, :])


def fused_kernel(
    R, Z, parts, count, x_hbm, table_hbm, seed_hbm, phase_hbm, t_hbm, coef_ref, low_ref, own,
    xs, table_ref, seed_ref, phase_ref, t_ref, f_ref, turned, acc, w, got, out, v, vgot, vout,
    gram, upper, lower, right, inverse, inner, send, recv, local, *rest
):
    phis, sems = rest[:parts], rest[parts:]
    r, z = lax.axis_index("rows"), lax.axis_index("rhs")
    size, panel = acc.shape[0], t_ref.shape[1]
    chunk = x_hbm.shape[1] // parts
    blocks = size // TILE
    wanted = [(seed_hbm, seed_ref), (phase_hbm, phase_ref), (table_hbm, table_ref)]
    wanted += [(x_hbm.at[:, i * chunk : (i + 1) * chunk], xs.at[z, i]) for i in range(parts)]
    wanted += [(t_hbm, t_ref)]
    loads = [pltpu.make_async_copy(*pair, local.at[i]) for i, pair in enumerate(wanted)]
    for load in loads:
        load.start()
    barrier = pltpu.get_barrier_semaphore()
    for d in range(1, R):
        pl.semaphore_signal(
            barrier, inc=1, device_id={"rows": lax.rem(r + d, R)}, device_id_type=MESH
        )
    for d in range(1, Z):
        pl.semaphore_signal(
            barrier, inc=1, device_id={"rhs": lax.rem(z + d, Z)}, device_id_type=MESH
        )
    pl.semaphore_wait(barrier, R + Z - 2)

    def moving(q, way):
        block, part = z - way * (q // parts), lax.rem(q, parts)
        if isinstance(q, int):
            source = x_hbm.at[:, q * chunk : (q + 1) * chunk]
        else:
            source = xs.at[block, part]
        return pltpu.make_async_remote_copy(
            src_ref=source,
            dst_ref=xs.at[block, part],
            send_sem=send.at[(way + 1) // 2, q],
            recv_sem=recv.at[(way + 1) // 2, q],
            device_id={"rhs": z + way},
            device_id_type=MESH,
        )

    def arriving(q, way):
        block, part = z - way * (q // parts + 1), lax.rem(q, parts)
        return pltpu.make_async_remote_copy(
            src_ref=xs.at[block, part],
            dst_ref=xs.at[block, part],
            send_sem=send.at[(way + 1) // 2, q],
            recv_sem=recv.at[(way + 1) // 2, q],
            device_id={"rhs": z - way},
            device_id_type=MESH,
        )

    def inside(p):
        return jnp.logical_and(p >= 0, p < Z)

    for q in range(parts):
        for way in (1, -1):
            pl.when(inside(z + way))(lambda: moving(q, way).start())
    for load in loads[:-1]:
        load.wait()
    f_ref[...] = pick(table_ref, seed_ref, phase_ref)
    loads[-1].wait()
    acc[...] = jnp.zeros_like(acc)
    near = jnp.minimum(z, Z - 1 - z)

    def visit(d):
        step = (d + 1) // 2
        both = jnp.where(d % 2 == 1, z - step, z + step)
        single = jnp.where(z < Z - 1 - z, z + d - near, z - d + near)
        return jnp.where(d <= 2 * near, both, single)

    def gather(part, block):
        acc[...] += jnp.dot(phis[part][block], turned[part], preferred_element_type=jnp.float32)

    phis[-1][z] = jnp.zeros(phis[-1].shape[1:], jnp.bfloat16)
    turned[parts - 1] = jnp.zeros(turned.shape[1:], jnp.bfloat16)

    @pl.loop(0, Z)
    def _(d):
        for part in range(parts):
            q = (d - 1) * parts + part
            for way in (1, -1):

                @pl.when(jnp.logical_and(d > 0, inside(z - way * d)))
                def _():
                    arriving(q, way).wait_recv()
                    pl.when(inside(z + way))(lambda: moving(q + parts, way).start())

        block = visit(d)
        gather(parts - 1, visit(jnp.maximum(d - 1, 0)))
        for part, phi in enumerate(phis):
            phi[block] = features(xs[block, part], f_ref[...])
            mine = phi[block, pl.ds(pl.multiple_of(z * panel, panel), panel), :]
            turned[part, :, :panel] = mine.T
            here = pl.multiple_of((block * parts + part) * chunk, chunk)
            turned[part, :, panel:] = t_ref[pl.ds(here, chunk), :]
            if part + 1 < parts:
                gather(part, block)

    gather(parts - 1, visit(Z - 1))
    stages = [
        exchange(
            R, Z, c * TILE // panel, count, w.at[c], got.at[c], out.at[c],
            [s.at[c] for s in sems[:8]],
        )
        for c in range(blocks)
    ]
    rows = TILE // R
    for c in range(blocks):
        for i in range(R):
            at = c * TILE + i * rows
            w[c, i] = acc[at : at + rows, :panel]
        stages[c][0]()
    high = size // R
    for i in range(R):
        v[i] = acc[i * high : (i + 1) * high, panel:]
    last = exchange(R, Z, 0, count, v, vgot, vout, sems[8:])
    last[0]()

    @pl.loop(0, Z * parts)
    def _(q):
        for way in (1, -1):
            sent = jnp.logical_and(inside(z + way), inside(z - way * (q // parts)))
            pl.when(sent)(lambda: moving(q, way).wait_send())

    def keep(part):
        own[part] = phis[part][z].T

    def spread(source, dest, base, height, first=0):
        for i in range(R):
            for j in range(first, Z):
                top = base + i * height
                dest[top : top + height, j * panel : (j + 1) * panel] = source[i, j]

    for step in (1, 2):
        for c in range(blocks):
            stages[c][step]()
    for part in range(parts):
        keep(part)
    stages[0][3]()
    last[1]()
    for c in range(1, blocks):
        stages[c][3]()
    stages[0][4]()
    spread(out.at[0], gram, 0, rows)
    row = lax.broadcasted_iota(jnp.int32, (TILE, TILE), 0)
    col = lax.broadcasted_iota(jnp.int32, (TILE, TILE), 1)
    eye = jnp.where(row == col, jnp.float32(ridge), 0.0)
    dot = exact

    def at(i):
        return slice(i * TILE, (i + 1) * TILE)

    @pl.loop(0, blocks)
    def _(k):
        mine = pl.ds(pl.multiple_of(k * TILE, TILE), TILE)

        @pl.loop(0, k)
        def _(i):
            above = pl.ds(pl.multiple_of(i * TILE, TILE), TILE)
            left = upper[above, mine].T
            lower[mine, above] = left
            gram[mine, :] -= dot(left, gram[above, :])

        upper[mine, :] = gram[mine, :]
        inner[...] = gram[mine, mine] + eye
        invert_block(inner, inverse.at[k])
        gram[mine, :] = dot(inverse[k], upper[mine, :])
        for c in range(1, blocks):

            @pl.when(k == c - 1)
            def _():
                stages[c][4]()
                spread(out.at[c], gram, c * TILE, rows, c * TILE // panel)

        for i, stage in ((0, last[2]), (2, last[3]), (3, last[4])):
            pl.when(k == min(i, blocks - 1))(stage)

    spread(vout, right, 0, high)
    for k in range(blocks):
        value = right[at(k), :]
        if k:
            value -= dot(lower[at(k), : k * TILE], right[: k * TILE, :])
        right[at(k), :] = dot(inverse[k], value)
    for k in reversed(range(blocks)):
        value = right[at(k), :]
        if k + 1 < blocks:
            value -= dot(gram[at(k), (k + 1) * TILE :], coef_ref[(k + 1) * TILE :, :])
        coef_ref[at(k), :] = value
        low_ref[at(k), :] = value.astype(jnp.bfloat16)


def fused(x, table, seeds, phases, targets):
    R, Z = lax.axis_size("rows"), lax.axis_size("rhs")
    depth, length = x.shape
    size = seeds.shape[1]
    panel = targets.shape[1]
    columns = Z * panel
    chunk = min(length, 512)
    parts = length // chunk
    blocks = size // TILE
    rows, high = TILE // R, size // R
    sems = pltpu.SemaphoreType.DMA
    f32, bf16 = jnp.float32, jnp.bfloat16
    place = lambda v: pltpu.with_memory_space_constraint(v, pltpu.HBM)
    return pl.pallas_call(
        functools.partial(fused_kernel, R, Z, parts, length * R * Z),
        out_shape=[
            pltpu.VMEM((size, columns), f32),
            pltpu.VMEM((size, columns), bf16),
            pltpu.VMEM((parts, chunk, size), bf16),
        ],
        in_specs=[HBM] * 5,
        out_specs=[VMEM, VMEM, VMEM],
        scratch_shapes=[
            pltpu.VMEM((Z, parts, depth, chunk), f32),
            pltpu.VMEM(table.shape, f32),
            pltpu.VMEM(seeds.shape, jnp.int32),
            pltpu.VMEM(phases.shape, f32),
            pltpu.VMEM(targets.shape, targets.dtype),
            pltpu.VMEM((size, 7 * depth), bf16),
            pltpu.VMEM((parts, chunk, 2 * panel), bf16),
            pltpu.VMEM((size, 2 * panel), f32),
            pltpu.VMEM((blocks, R, rows, panel), f32),
            pltpu.VMEM((blocks, R, rows, panel), f32),
            pltpu.VMEM((blocks, R, Z, rows, panel), f32),
            pltpu.VMEM((R, high, panel), f32),
            pltpu.VMEM((R, high, panel), f32),
            pltpu.VMEM((R, Z, high, panel), f32),
            pltpu.VMEM((size, size), f32),
            pltpu.VMEM((size, size), f32),
            pltpu.VMEM((size, size), f32),
            pltpu.VMEM((size, columns), f32),
            pltpu.VMEM((blocks, TILE, TILE), f32),
            pltpu.VMEM((TILE, TILE), f32),
            sems((2, Z * parts)),
            sems((2, Z * parts)),
            sems((4 + parts,)),
        ]
        + [pltpu.VMEM((Z, size, chunk), bf16)] * parts
        + [sems((blocks, R))] * 2 + [sems((blocks, Z))] * 2 + [sems((blocks, R))] * 4
        + [sems((R,))] * 2 + [sems((Z,))] * 2 + [sems((R,))] * 4,
        compiler_params=pltpu.CompilerParams(collective_id=0, has_side_effects=True, vmem_limit_bytes=40 << 20),
    )(*map(place, (x, table, seeds, phases, targets)))


def fit_kernel(own_ref, low_ref, coef_ref, coef_out, fitted_out, fitted, sems):
    parts, chunk = own_ref.shape[:2]
    copies = [pltpu.make_async_copy(coef_ref, coef_out, sems.at[0])]
    copies[0].start()
    half = chunk // 2
    for part in range(parts):
        for side in range(2):
            rows = slice(side * half, (side + 1) * half)
            fitted[part, rows, :] = jnp.dot(
                own_ref[part, rows, :], low_ref[...], preferred_element_type=jnp.float32
            )
            i = 2 * part + side
            copies.append(
                pltpu.make_async_copy(
                    fitted.at[part, rows], fitted_out.at[part, rows], sems.at[1 + i]
                )
            )
            copies[-1].start()
    for copy in copies:
        copy.wait()


def fit(own, low, coef):
    parts, chunk, size = own.shape
    columns = low.shape[1]
    shape = (parts, chunk, columns)
    return pl.pallas_call(
        fit_kernel,
        in_specs=[VMEM, VMEM, VMEM],
        out_specs=[ANY, ANY],
        out_shape=[
            jax.ShapeDtypeStruct((size, columns), jnp.float32),
            jax.ShapeDtypeStruct(shape, jnp.float32),
        ],
        scratch_shapes=[
            pltpu.VMEM(shape, jnp.float32),
            pltpu.SemaphoreType.DMA((1 + 2 * parts,)),
        ],
        compiler_params=pltpu.CompilerParams(vmem_limit_bytes=16 << 20),
    )(own, low, coef)


def body(samples, freq_table, feature_seeds, phases, treatment_features):
    seeds, shifts = feature_seeds.reshape(1, -1), phases.reshape(1, -1)
    coef, low_coef, own = fused(samples.T, freq_table.T, seeds, shifts, treatment_features)
    coefficients, fitted = fit(own, low_coef, coef)
    return (coefficients, fitted.reshape(samples.shape[0], low_coef.shape[1]))


def solution(mesh):
    placed = (P(("rows", "rhs"), None), P(), P(), P(), P("rows", "rhs"))
    return jax.shard_map(
        body, mesh=mesh, in_specs=placed, out_specs=(P(), P(("rows", "rhs"), None)), check_vma=False
    )
```

```python
import functools
import math

import jax
import jax.numpy as jnp
from jax import lax
from jax.experimental import pallas as pl
from jax.experimental.pallas import tpu as pltpu
from jax.sharding import PartitionSpec as P

ridge = 0.05
MESH = pl.DeviceIdType.MESH
HIGHEST = lax.Precision.HIGHEST
VMEM = pl.BlockSpec(memory_space=pltpu.VMEM)
ANY = pl.BlockSpec(memory_space=pl.ANY)
HBM = pl.BlockSpec(memory_space=pltpu.HBM)
TILE = 128
SIN_TERMS = [3.141592580044735, -5.1677068789267455, 2.550031377285281, -0.598045174146624, 0.07722012899537994]


def split(x):
    high = x.astype(jnp.bfloat16)
    rest = x - high.astype(jnp.float32)
    middle = rest.astype(jnp.bfloat16)
    low = (rest - middle.astype(jnp.float32)).astype(jnp.bfloat16)
    return high, middle, low


def exact(a, b):
    ah, am, al = split(a)
    bh, bm, bl = split(b)
    return jnp.dot(
        jnp.concatenate([am, al, am, ah, ah, ah], axis=1),
        jnp.concatenate([bm, bh, bh, bl, bm, bh], axis=0),
        preferred_element_type=jnp.float32,
    )


def pick(table_ref, seed_ref, phase_ref):
    turn = jnp.float32(1.0 / (2.0 * math.pi))
    depth, length = table_ref.shape
    size = seed_ref.shape[1]
    tile = min(length, 512)
    stack = jnp.concatenate(split(table_ref[...] * turn), axis=0)
    row = lax.broadcasted_iota(jnp.int32, (tile, size), 0)
    found = jnp.zeros((3 * depth, size), jnp.float32)
    for k in range(0, length, tile):
        chosen = jnp.where(row == seed_ref[...] - k, 1.0, 0.0).astype(jnp.bfloat16)
        found += jnp.dot(stack[:, k : k + tile], chosen, preferred_element_type=jnp.float32)
    high, middle, low = (found[i * depth : (i + 1) * depth] for i in range(3))
    shift = [t.astype(jnp.float32) for t in split(phase_ref[...] * turn)]
    shift = jnp.concatenate(shift + [jnp.zeros((depth - 3, size), jnp.float32)], axis=0)
    full = jnp.concatenate([high, middle, high, middle, low, high, shift], axis=0)
    return full.T.astype(jnp.bfloat16)


def features(x, f):
    high, middle, low = split(x)
    ones = jnp.ones(x.shape, jnp.bfloat16)
    rows = jnp.concatenate([high, high, middle, middle, high, low, ones], axis=0)
    turns = jnp.dot(f, rows, preferred_element_type=jnp.float32)
    r = turns - jnp.round(turns)
    u = r * r
    scale = math.sqrt(2.0 * math.sqrt(2.0))
    s = u * (SIN_TERMS[-1] * scale) + SIN_TERMS[-2] * scale
    for term in reversed(SIN_TERMS[:-2]):
        s = s * u + term * scale
    s = s * r
    return (math.sqrt(2.0) - s * s).astype(jnp.bfloat16)


def exchange(R, Z, low, count, w_ref, got, out, sems):
    send, recv, zsend, zrecv, psend, precv, csend, crecv = sems
    r, z = lax.axis_index("rows"), lax.axis_index("rhs")
    core, spot, half = lax.rem(r, 2), r // 2, R // 2

    def holds(column):
        return (lambda f: f()) if low == 0 else pl.when(column >= low)

    def copy(src, dst, out_sem, in_sem, d, peer):
        return pltpu.make_async_remote_copy(
            src_ref=src,
            dst_ref=dst,
            send_sem=out_sem.at[d],
            recv_sem=in_sem.at[d],
            device_id=peer,
            device_id_type=MESH,
        )

    def scatter(d):
        peer = lax.rem(r + d, R)
        return copy(w_ref.at[peer], got.at[d], send, recv, d, {"rows": peer})

    def along(d):
        mine = out.at[r, z]
        return copy(mine, mine, zsend, zrecv, d, {"rhs": lax.rem(z + d, Z)})

    def across(d):
        peer = lax.rem(spot + d, half) * 2 + core
        where = out.at[r, low:]
        return copy(where, where, psend, precv, d, {"rows": peer})

    def aside(d):
        where = out.at[lax.rem(spot - d + half, half) * 2 + core, low:]
        return copy(where, where, csend, crecv, d, {"rows": r + 1 - 2 * core})

    def first():
        @holds(z)
        def _():
            for d in range(1, R):
                scatter(d).start()

    def second():
        @holds(z)
        def _():
            total = w_ref[r]
            for d in range(1, R):
                scatter(d).wait()
                total = total + got[d]
            out[r, z] = total * (1.0 / count)
            for d in range(1, Z):
                along(d).start()

    def third():
        for d in range(1, Z):
            holds(lax.rem(z - d + Z, Z))(along(d).wait_recv)
        for d in range(1, half):
            across(d).start()
        aside(0).start()

    def fourth():
        for d in range(1, half):
            across(d).wait()
            aside(d).start()

    def last():
        for d in range(half):
            aside(d).wait()

        @holds(z)
        def _():
            for d in range(1, Z):
                along(d).wait_send()

    return first, second, third, fourth, last


def sweep(a, base):
    shape = a[0].shape
    lane = lax.broadcasted_iota(jnp.int32, shape, 1)
    sub = lax.broadcasted_iota(jnp.int32, shape, 0)

    def across(v, j):
        return jnp.broadcast_to(v[:, j : j + 1], shape)

    def down(v, i):
        return jnp.broadcast_to(v[i : i + 1, :], shape)

    for g in range(len(a)):
        k = base + 8 * g
        c = [0.0 - across(a[g], k + j) for j in range(8)]
        far = [[across(v, k + j) if i != g else None for i, v in enumerate(a)] for j in range(8)]
        inside = jnp.logical_and(lane >= k, lane < k + 8)
        rows = jnp.where(inside, jnp.where(lane == sub + k, 1.0, 0.0), a[g])
        for s in range(0, 8, 2):
            p, q, r = down(c[s], s), down(c[s + 1], s), down(c[s + 1], s + 1)
            scale = 1.0 / (p * r - q * q)
            pair = jnp.logical_and(sub >= s, sub < s + 2)
            l0 = jnp.where(pair, jnp.where(sub == s, 1.0, 0.0), c[s])
            l1 = jnp.where(pair, jnp.where(sub == s, 0.0, 1.0), c[s + 1])

            def step(v):
                v0, v1 = down(v, s), down(v, s + 1)
                u0, u1 = r * v0 - q * v1, p * v1 - q * v0
                return jnp.where(pair, 0.0, v) - scale * (l0 * u0 + l1 * u1)

            rows = step(rows)
            for j in range(s + 2, 8):
                c[j] = step(c[j])
        w = [down(rows, i) for i in range(8)]
        for i in range(len(a)):
            if i == g:
                continue
            f = [far[j][i] * w[j] for j in range(8)]
            total = ((f[0] + f[1]) + (f[2] + f[3])) + ((f[4] + f[5]) + (f[6] + f[7]))
            a[i] = jnp.where(inside, 0.0, a[i]) - total
        a[g] = rows
    return a


def invert_block(ref, dst):
    half = TILE // 2
    groups = half // 8
    dot = functools.partial(jnp.dot, precision=HIGHEST, preferred_element_type=jnp.float32)
    left = lax.broadcasted_iota(jnp.int32, (half, TILE), 1) < half
    top = sweep([ref[8 * i : 8 * i + 8, :] for i in range(groups)], 0)
    for i in range(groups):
        dst[8 * i : 8 * i + 8, :] = top[i]
    lower = ref[half:, :]
    lower = jnp.where(left, 0.0, lower) - dot(lower[:, :half], dst[:half, :])
    low = sweep([lower[8 * i : 8 * i + 8, :] for i in range(groups)], half)
    for i in range(groups):
        dst[half + 8 * i : half + 8 * i + 8, :] = low[i]
    upper = dst[:half, :]
    dst[:half, :] = jnp.where(left, upper, 0.0) - dot(upper[:, half:], dst[half:, :])


def fused_kernel(
    R, Z, parts, count, x_hbm, table_hbm, seed_hbm, phase_hbm, t_hbm, coef_ref, low_ref, own,
    xs, table_ref, seed_ref, phase_ref, t_ref, f_ref, turned, acc, w, got, out, v, vgot, vout,
    gram, upper, lower, right, inverse, inner, send, recv, local, *rest
):
    phis, sems = rest[:parts], rest[parts:]
    r, z = lax.axis_index("rows"), lax.axis_index("rhs")
    size, panel = acc.shape[0], t_ref.shape[1]
    chunk = x_hbm.shape[1] // parts
    blocks = size // TILE
    wanted = [(seed_hbm, seed_ref), (phase_hbm, phase_ref), (table_hbm, table_ref)]
    wanted += [(x_hbm.at[:, i * chunk : (i + 1) * chunk], xs.at[z, i]) for i in range(parts)]
    wanted += [(t_hbm, t_ref)]
    loads = [pltpu.make_async_copy(*pair, local.at[i]) for i, pair in enumerate(wanted)]
    for load in loads:
        load.start()
    barrier = pltpu.get_barrier_semaphore()
    for d in range(1, R):
        pl.semaphore_signal(
            barrier, inc=1, device_id={"rows": lax.rem(r + d, R)}, device_id_type=MESH
        )
    for d in range(1, Z):
        pl.semaphore_signal(
            barrier, inc=1, device_id={"rhs": lax.rem(z + d, Z)}, device_id_type=MESH
        )
    pl.semaphore_wait(barrier, R + Z - 2)

    def moving(q, way):
        block, part = z - way * (q // parts), lax.rem(q, parts)
        if isinstance(q, int):
            source = x_hbm.at[:, q * chunk : (q + 1) * chunk]
        else:
            source = xs.at[block, part]
        return pltpu.make_async_remote_copy(
            src_ref=source,
            dst_ref=xs.at[block, part],
            send_sem=send.at[(way + 1) // 2, q],
            recv_sem=recv.at[(way + 1) // 2, q],
            device_id={"rhs": z + way},
            device_id_type=MESH,
        )

    def arriving(q, way):
        block, part = z - way * (q // parts + 1), lax.rem(q, parts)
        return pltpu.make_async_remote_copy(
            src_ref=xs.at[block, part],
            dst_ref=xs.at[block, part],
            send_sem=send.at[(way + 1) // 2, q],
            recv_sem=recv.at[(way + 1) // 2, q],
            device_id={"rhs": z - way},
            device_id_type=MESH,
        )

    def inside(p):
        return jnp.logical_and(p >= 0, p < Z)

    for q in range(parts):
        for way in (1, -1):
            pl.when(inside(z + way))(lambda: moving(q, way).start())
    for load in loads[:-1]:
        load.wait()
    f_ref[...] = pick(table_ref, seed_ref, phase_ref)
    loads[-1].wait()
    acc[...] = jnp.zeros_like(acc)
    near = jnp.minimum(z, Z - 1 - z)

    def visit(d):
        step = (d + 1) // 2
        both = jnp.where(d % 2 == 1, z - step, z + step)
        single = jnp.where(z < Z - 1 - z, z + d - near, z - d + near)
        return jnp.where(d <= 2 * near, both, single)

    def gather(part, block):
        acc[...] += jnp.dot(phis[part][block], turned[part], preferred_element_type=jnp.float32)

    phis[-1][z] = jnp.zeros(phis[-1].shape[1:], jnp.bfloat16)
    turned[parts - 1] = jnp.zeros(turned.shape[1:], jnp.bfloat16)

    @pl.loop(0, Z)
    def _(d):
        for part in range(parts):
            q = (d - 1) * parts + part
            for way in (1, -1):

                @pl.when(jnp.logical_and(d > 0, inside(z - way * d)))
                def _():
                    arriving(q, way).wait_recv()
                    pl.when(inside(z + way))(lambda: moving(q + parts, way).start())

        block = visit(d)
        gather(parts - 1, visit(jnp.maximum(d - 1, 0)))
        for part, phi in enumerate(phis):
            phi[block] = features(xs[block, part], f_ref[...])
            mine = phi[block, pl.ds(pl.multiple_of(z * panel, panel), panel), :]
            turned[part, :, :panel] = mine.T
            here = pl.multiple_of((block * parts + part) * chunk, chunk)
            turned[part, :, panel:] = t_ref[pl.ds(here, chunk), :]
            if part + 1 < parts:
                gather(part, block)

    gather(parts - 1, visit(Z - 1))
    stages = [
        exchange(
            R, Z, c * TILE // panel, count, w.at[c], got.at[c], out.at[c],
            [s.at[c] for s in sems[:8]],
        )
        for c in range(blocks)
    ]
    rows = TILE // R
    for c in range(blocks):
        for i in range(R):
            at = c * TILE + i * rows
            w[c, i] = acc[at : at + rows, :panel]
        stages[c][0]()
    high = size // R
    for i in range(R):
        v[i] = acc[i * high : (i + 1) * high, panel:]
    last = exchange(R, Z, 0, count, v, vgot, vout, sems[8:])
    last[0]()

    @pl.loop(0, Z * parts)
    def _(q):
        for way in (1, -1):
            sent = jnp.logical_and(inside(z + way), inside(z - way * (q // parts)))
            pl.when(sent)(lambda: moving(q, way).wait_send())

    def keep(part):
        own[part] = phis[part][z].T

    def spread(source, dest, base, height, first=0):
        for i in range(R):
            for j in range(first, Z):
                top = base + i * height
                dest[top : top + height, j * panel : (j + 1) * panel] = source[i, j]

    for step in (1, 2):
        for c in range(blocks):
            stages[c][step]()
    for part in range(parts):
        keep(part)
    stages[0][3]()
    last[1]()
    for c in range(1, blocks):
        stages[c][3]()
    stages[0][4]()
    spread(out.at[0], gram, 0, rows)
    row = lax.broadcasted_iota(jnp.int32, (TILE, TILE), 0)
    col = lax.broadcasted_iota(jnp.int32, (TILE, TILE), 1)
    eye = jnp.where(row == col, jnp.float32(ridge), 0.0)
    dot = exact

    def at(i):
        return slice(i * TILE, (i + 1) * TILE)

    for k in range(blocks):
        ahead = slice(k * TILE, size)
        value = gram[at(k), ahead]
        if k:
            left = upper[: k * TILE, at(k)].T
            lower[at(k), : k * TILE] = left
            value -= dot(left, gram[: k * TILE, ahead])
        upper[at(k), ahead] = value
        inner[...] = value[:, :TILE] + eye
        invert_block(inner, inverse.at[k])
        if k + 1 < blocks:
            after = slice((k + 1) * TILE, size)
            gram[at(k), after] = dot(inverse[k], upper[at(k), after])
            stages[k + 1][4]()
            spread(out.at[k + 1], gram, (k + 1) * TILE, rows, (k + 1) * TILE // panel)
        for i, stage in ((0, last[2]), (2, last[3]), (3, last[4])):
            if k == min(i, blocks - 1):
                stage()

    spread(vout, right, 0, high)
    for k in range(blocks):
        value = right[at(k), :]
        if k:
            value -= dot(lower[at(k), : k * TILE], right[: k * TILE, :])
        right[at(k), :] = dot(inverse[k], value)
    for k in reversed(range(blocks)):
        value = right[at(k), :]
        if k + 1 < blocks:
            value -= dot(gram[at(k), (k + 1) * TILE :], coef_ref[(k + 1) * TILE :, :])
        coef_ref[at(k), :] = value
        low_ref[at(k), :] = value.astype(jnp.bfloat16)


def fused(x, table, seeds, phases, targets):
    R, Z = lax.axis_size("rows"), lax.axis_size("rhs")
    depth, length = x.shape
    size = seeds.shape[1]
    panel = targets.shape[1]
    columns = Z * panel
    chunk = min(length, 512)
    parts = length // chunk
    blocks = size // TILE
    rows, high = TILE // R, size // R
    sems = pltpu.SemaphoreType.DMA
    f32, bf16 = jnp.float32, jnp.bfloat16
    place = lambda v: pltpu.with_memory_space_constraint(v, pltpu.HBM)
    return pl.pallas_call(
        functools.partial(fused_kernel, R, Z, parts, length * R * Z),
        out_shape=[
            pltpu.VMEM((size, columns), f32),
            pltpu.VMEM((size, columns), bf16),
            pltpu.VMEM((parts, chunk, size), bf16),
        ],
        in_specs=[HBM] * 5,
        out_specs=[VMEM, VMEM, VMEM],
        scratch_shapes=[
            pltpu.VMEM((Z, parts, depth, chunk), f32),
            pltpu.VMEM(table.shape, f32),
            pltpu.VMEM(seeds.shape, jnp.int32),
            pltpu.VMEM(phases.shape, f32),
            pltpu.VMEM(targets.shape, targets.dtype),
            pltpu.VMEM((size, 7 * depth), bf16),
            pltpu.VMEM((parts, chunk, 2 * panel), bf16),
            pltpu.VMEM((size, 2 * panel), f32),
            pltpu.VMEM((blocks, R, rows, panel), f32),
            pltpu.VMEM((blocks, R, rows, panel), f32),
            pltpu.VMEM((blocks, R, Z, rows, panel), f32),
            pltpu.VMEM((R, high, panel), f32),
            pltpu.VMEM((R, high, panel), f32),
            pltpu.VMEM((R, Z, high, panel), f32),
            pltpu.VMEM((size, size), f32),
            pltpu.VMEM((size, size), f32),
            pltpu.VMEM((size, size), f32),
            pltpu.VMEM((size, columns), f32),
            pltpu.VMEM((blocks, TILE, TILE), f32),
            pltpu.VMEM((TILE, TILE), f32),
            sems((2, Z * parts)),
            sems((2, Z * parts)),
            sems((4 + parts,)),
        ]
        + [pltpu.VMEM((Z, size, chunk), bf16)] * parts
        + [sems((blocks, R))] * 2 + [sems((blocks, Z))] * 2 + [sems((blocks, R))] * 4
        + [sems((R,))] * 2 + [sems((Z,))] * 2 + [sems((R,))] * 4,
        compiler_params=pltpu.CompilerParams(collective_id=0, has_side_effects=True, vmem_limit_bytes=40 << 20),
    )(*map(place, (x, table, seeds, phases, targets)))


def fit_kernel(own_ref, low_ref, coef_ref, coef_out, fitted_out, fitted, sems):
    parts, chunk = own_ref.shape[:2]
    copies = [pltpu.make_async_copy(coef_ref, coef_out, sems.at[0])]
    copies[0].start()
    half = chunk // 2
    for part in range(parts):
        for side in range(2):
            rows = slice(side * half, (side + 1) * half)
            fitted[part, rows, :] = jnp.dot(
                own_ref[part, rows, :], low_ref[...], preferred_element_type=jnp.float32
            )
            i = 2 * part + side
            copies.append(
                pltpu.make_async_copy(
                    fitted.at[part, rows], fitted_out.at[part, rows], sems.at[1 + i]
                )
            )
            copies[-1].start()
    for copy in copies:
        copy.wait()


def fit(own, low, coef):
    parts, chunk, size = own.shape
    columns = low.shape[1]
    shape = (parts, chunk, columns)
    return pl.pallas_call(
        fit_kernel,
        in_specs=[VMEM, VMEM, VMEM],
        out_specs=[ANY, ANY],
        out_shape=[
            jax.ShapeDtypeStruct((size, columns), jnp.float32),
            jax.ShapeDtypeStruct(shape, jnp.float32),
        ],
        scratch_shapes=[
            pltpu.VMEM(shape, jnp.float32),
            pltpu.SemaphoreType.DMA((1 + 2 * parts,)),
        ],
        compiler_params=pltpu.CompilerParams(vmem_limit_bytes=16 << 20),
    )(own, low, coef)


def body(samples, freq_table, feature_seeds, phases, treatment_features):
    seeds, shifts = feature_seeds.reshape(1, -1), phases.reshape(1, -1)
    coef, low_coef, own = fused(samples.T, freq_table.T, seeds, shifts, treatment_features)
    coefficients, fitted = fit(own, low_coef, coef)
    return (coefficients, fitted.reshape(samples.shape[0], low_coef.shape[1]))


def solution(mesh):
    placed = (P(("rows", "rhs"), None), P(), P(), P(), P("rows", "rhs"))
    return jax.shard_map(
        body, mesh=mesh, in_specs=placed, out_specs=(P(), P(("rows", "rhs"), None)), check_vma=False
    )
```
